128 devices in a mesh: lat: 8 (over z, core), lon: 16 (over y, x).
Axes of the slice: x: 4, y: 4, z: 4, core: 2. Of those that a mesh axis runs over, the one named last changes fastest.
Arguments:
- ice_state: float32 [5, 2048, 4096], P(None, 'lat', 'lon'), may hold values from -6 to 6
- ocean_forcing: float32 [4, 2048, 4096], P(None, 'lat', 'lon'), may hold values from -6 to 6
- ice_strength: float32 [2048, 4096], P('lat', 'lon'), may hold values from 0.5 to 4
- ice_mask: int32 [2048, 4096], P('lat', 'lon'), may hold values from 0 to 1, as said below
- yield_mask: int32 [6, 2048, 4096], P(None, 'lat', 'lon'), may hold values 0 or 1
- ice_route: int32 [8, 8], replicated, may hold values from 0 to 7, each once within a row
Outputs:
- ocean_flux: float32 [2, 2048, 4096], P(None, 'lat', 'lon')
- ice_blocks: float32 [64, 5, 32, 4096], P('lat', None, None, 'lon')
The draws below stay inside these ranges and needn't reach their ends.
Inputs may be any that keep to these rules, and one draw needn't show every extreme that they name: `ice_route`: each row is a permutation of 0 .. 7. `ice_mask`: ice is set block by block of 32 latitude rows: every block of the first and of the last latitude band may hold ice, and one or more blocks of every other band; in all other blocks it is 0.
All inputs are finite; a program needn't handle non-finite values. No bound on the sum of `yield_mask` on one device may be relied on, other than what follows from the above.
Results may differ from the reference program's by a relative error of at most 0.00011.
Values sent between devices are 32-bit elements; how exact they have to be, the bound alone decides.
A program may use at most 128 MiB of HBM per device.

```python
import math
import jax
import jax.numpy as jnp

BY = 32
SUB = 6
CY = 256
NLAT = 2048
NLON = 4096
N_LAT = 8


def draw_ice_mask(key, part):
    per_band = CY // BY
    bands = NLAT // CY
    block_count = NLAT // BY
    first, second, third = jax.random.split(key, 3)
    blocks = jnp.arange(block_count, dtype=jnp.int32)
    band_of = blocks // per_band
    within = blocks % per_band
    coins = jax.random.randint(first, (block_count,), 0, 4)
    chosen = jax.random.randint(second, (bands,), 0, per_band)
    icy_block = (band_of == 0) | (band_of == bands - 1) | (coins == 0) | (within == chosen[band_of])
    rows = jnp.arange(NLAT, dtype=jnp.int32) // BY
    icy_rows = icy_block[rows]
    cells = jax.random.randint(third, (NLAT, NLON), 0, 5)
    return jnp.where(icy_rows[:, None] & (cells > 0), 1, 0).astype(jnp.int32)


def touch_ends(values, rng, least, top_value):
    shape = values.shape
    place = [jax.random.randint(jax.random.fold_in(rng, axis), (), 0, shape[axis]) for axis in range(len(shape))]
    values = values.at[tuple(place)].set(least)
    longest = shape.index(max(shape))
    place[longest] = (place[longest] + 1) % shape[longest]
    return values.at[tuple(place)].set(top_value)


def levels(key, extent, shards, smallest, high):
    factor_of = 1.0
    for axis_at, shards_of in shards:
        draws = jax.random.uniform(jax.random.fold_in(jax.random.fold_in(key, 6), axis_at), (shards_of,), jnp.float32, smallest / len(shards), high / len(shards))
        factor_of = factor_of * jnp.repeat(jnp.exp(draws), extent[axis_at] // shards_of).reshape((-1,) + (1,) * (len(extent) - 1 - axis_at))
    return factor_of


def noise(rng, shape, spread, reach, cuts=(), kind=jnp.bfloat16):
    level = levels(rng, shape, cuts, -0.22, 0.18) if cuts else 1.0
    array = jax.random.normal(rng, shape, jnp.float32) * spread * level
    return jnp.minimum(jnp.maximum(array, -reach), reach).astype(kind)


def setup_inputs(seed: int = 0) -> dict:
    keys = jax.random.split(jax.random.key(seed), 7)
    ice_state = noise(keys[0], (5, NLAT, NLON), 1.0, 6.0, ((1, 8), (2, 16)), jnp.float32)
    ocean_forcing = noise(keys[1], (4, NLAT, NLON), 1.0, 6.0, ((1, 8), (2, 16)), jnp.float32)
    ice_strength = jnp.clip(jnp.exp(math.log(4.0) - 2.0794415 * jax.random.uniform(keys[2], (NLAT, NLON), jnp.float32) ** levels(keys[2], (NLAT, NLON), ((0, 8), (1, 16)), -0.2, 0.2)), 0.5, 4.0)
    ice_mask = draw_ice_mask(jax.random.fold_in(keys[6], 71), 0)
    yield_mask = touch_ends((jax.random.randint(keys[4], (SUB, NLAT, NLON), 0, 2) < 1).astype(jnp.int32), jax.random.fold_in(keys[4], 1), 0, 1)
    ice_route = jax.vmap(lambda own: jax.random.permutation(own, N_LAT))(jax.random.split(keys[5], N_LAT)).reshape((N_LAT, N_LAT)).astype(jnp.int32)
    return dict(ice_state=ice_state, ocean_forcing=ocean_forcing, ice_strength=ice_strength, ice_mask=ice_mask, yield_mask=yield_mask, ice_route=ice_route)


RELAX_RATE = 1.0
STEP_WEIGHT = 0.5
DRAG_COEF = 0.5
CORIOLIS = 0.3


def inner(field, depth):
    return field[..., depth:field.shape[-2] - depth, depth:field.shape[-1] - depth]


def subcycle(state, forcing, ice, regime):
    velo_x, velo_y = state[0], state[1]
    stretch_x = (velo_x[1:-1, 2:] - velo_x[1:-1, :-2]) * 0.5
    stretch_y = (velo_y[2:, 1:-1] - velo_y[:-2, 1:-1]) * 0.5
    cross_x = (velo_x[2:, 1:-1] - velo_x[:-2, 1:-1]) * 0.5
    cross_y = (velo_y[1:-1, 2:] - velo_y[1:-1, :-2]) * 0.5
    strength = inner(forcing[4], 1)
    ice_one = inner(ice, 1)
    viscous = strength * (1.5 - inner(regime, 1))
    keep = 1.0 / (1.0 + RELAX_RATE)
    new_sum = ice_one * (inner(state[2], 1) + RELAX_RATE * (viscous * (stretch_x + stretch_y) - 0.5 * strength)) * keep
    new_diff = ice_one * (inner(state[3], 1) + RELAX_RATE * 0.5 * viscous * (stretch_x - stretch_y)) * keep
    new_shear = ice_one * (inner(state[4], 1) + RELAX_RATE * 0.25 * viscous * (cross_x + cross_y)) * keep
    normal_x = new_sum + new_diff
    normal_y = new_sum - new_diff
    force_x = (normal_x[1:-1, 2:] - normal_x[1:-1, :-2]) * 0.25 + (new_shear[2:, 1:-1] - new_shear[:-2, 1:-1]) * 0.5
    force_y = (normal_y[2:, 1:-1] - normal_y[:-2, 1:-1]) * 0.25 + (new_shear[1:-1, 2:] - new_shear[1:-1, :-2]) * 0.5
    ice_two = inner(ice, 2)
    old_x = inner(velo_x, 2)
    old_y = inner(velo_y, 2)
    damp = 1.0 / (1.0 + STEP_WEIGHT * DRAG_COEF)
    next_x = ice_two * (old_x + STEP_WEIGHT * (force_x + inner(forcing[0], 2) + DRAG_COEF * inner(forcing[2], 2) + CORIOLIS * old_y)) * damp
    next_y = ice_two * (old_y + STEP_WEIGHT * (force_y + inner(forcing[1], 2) + DRAG_COEF * inner(forcing[3], 2) - CORIOLIS * old_x)) * damp
    return jnp.stack([next_x, next_y, inner(new_sum, 1), inner(new_diff, 1), inner(new_shear, 1)])


def evolve(state, forcing, ice, regimes):
    for level in range(regimes.shape[0]):
        trim = 2 * level
        state = subcycle(state, inner(forcing, trim), inner(ice, trim), inner(regimes[level], trim))
    return state


def reference(ice_state, ocean_forcing, ice_strength, ice_mask, yield_mask, ice_route):
    depth = 2 * SUB

    def widen(field):
        field = jnp.concatenate([field[..., -depth:], field, field[..., :depth]], axis=-1)
        widths = [(0, 0)] * (field.ndim - 2) + [(depth, depth), (0, 0)]
        return jnp.pad(field, widths)

    forcing = jnp.concatenate([ocean_forcing, ice_strength[None]], axis=0)
    ice_f = ice_mask.astype(jnp.float32)
    final = evolve(widen(ice_state), widen(forcing), widen(ice_f), widen(yield_mask.astype(jnp.float32)))
    ocean_flux = DRAG_COEF * ice_f[None] * (final[:2] - ocean_forcing[2:4])
    blocks = final.reshape(5, N_LAT, N_LAT, BY, NLON)
    lanes = jnp.arange(N_LAT, dtype=jnp.int32)
    match = (ice_route[:, :, None] == lanes[None, None, :]).astype(jnp.int32)
    inverse = jnp.sum(match * lanes[None, :, None], axis=1)
    source = jnp.broadcast_to(lanes[None, :], (N_LAT, N_LAT))
    picked = blocks[:, source, inverse.T]
    ice_blocks = picked.transpose(1, 2, 0, 3, 4).reshape(N_LAT * N_LAT, 5, BY, NLON)
    return ocean_flux, ice_blocks
```

```python
import functools

import jax
import jax.numpy as jnp
from jax import lax
from jax.experimental import pallas as pl
from jax.experimental.pallas import tpu as pltpu
from jax.sharding import PartitionSpec as P

RELAX_RATE = 1.0
STEP_WEIGHT = 0.5
DRAG_COEF = 0.5
CORIOLIS = 0.3

KEEP = 1.0 / (1.0 + RELAX_RATE)
DAMP = 1.0 / (1.0 + STEP_WEIGHT * DRAG_COEF)

MESH = pl.DeviceIdType.MESH
LANES = 128
SUBLANES = 8
RIM = 16
EDGE = RIM // SUBLANES

U, V, A, B, T, Q, GX, GY, C = range(9)


def layout(count):
    deep = 2 * count
    widths = {U: deep, V: deep, A: deep - 1, T: deep - 1, Q: deep - 1}
    for level in range(count):
        widths[C + level] = deep - 1 - 2 * level
    widths.update({B: deep - 2, GX: deep - 2, GY: deep - 2})
    places, at = {}, 0
    for field in widths:
        places[field] = at
        at += widths[field]
    assert at <= LANES
    return widths, places


def spin(cells, shift):
    shift = shift % LANES
    return cells if shift == 0 else pltpu.roll(cells, shift, 1)


def kernel(
    count,
    lats,
    lons,
    route,
    state,
    forcing,
    strength,
    mask,
    regime,
    flux,
    blocks,
    ext,
    raw_stress,
    raw_force,
    raw_strength,
    raw_mask,
    raw_regime,
    pack_west,
    pack_east,
    rim_east,
    rim_west,
    work_u,
    work_v,
    work_a,
    work_b,
    work_t,
    edge,
    outbox,
    order,
    load_sem,
    rim_send,
    rim_recv,
    route_send,
    route_recv,
    own_sem,
):
    fields = C + count
    widths, places = layout(count)
    groups = state.shape[1]
    rows = groups * SUBLANES
    block_rows = rows // lats
    span = block_rows + 2 * RIM
    me = lax.axis_index("lat")
    here = lax.axis_index("lon")
    west = lax.rem(here + lons - 1, lons)
    east = lax.rem(here + 1, lons)
    north = lax.rem(me + lats - 1, lats)
    south = lax.rem(me + 1, lats)

    barrier = pltpu.get_barrier_semaphore()
    greeted = 0
    for step in range(1, lats):
        pl.semaphore_signal(
            barrier, inc=1, device_id=(lax.rem(me + step, lats), here), device_id_type=MESH
        )
        greeted += 1
    for lon in (west, east):
        for lat in (north, me, south):
            pl.semaphore_signal(barrier, inc=1, device_id=(lat, lon), device_id_type=MESH)
            greeted += 1

    loads = []

    def load(src, dst):
        copy = pltpu.make_async_copy(src, dst, load_sem.at[len(loads)])
        copy.start()
        loads.append(copy)

    for tile in range(2):
        lanes = pl.ds(tile * LANES, LANES)
        load(state.at[pl.ds(0, 2), :, :, lanes], ext.at[pl.ds(0, 2), tile, pl.ds(EDGE, groups)])
        load(state.at[pl.ds(2, 3), :, :, lanes], raw_stress.at[:, tile])
        load(forcing.at[:, :, :, lanes], raw_force.at[:, tile])
        load(strength.at[:, :, lanes], raw_strength.at[tile])
        load(mask.at[:, :, lanes], raw_mask.at[tile])
        load(regime.at[:, :, :, lanes], raw_regime.at[:, tile])

    for lat in range(lats):
        block = jnp.int32(0)
        for j in range(1, lats):
            apart = route[me, j] - lat
            block = block + j * (1 - lax.div(apart * apart + 63, 64))
        order[lat] = lax.rem(block, lats)
    for copy in loads:
        copy.wait()

    lane = lax.broadcasted_iota(jnp.int32, (8, LANES), 1)

    def prepare(at, _):
        inside = at + EDGE
        packs = []
        for tile in range(2):
            ice = raw_mask[tile, at].astype(jnp.float32)
            firm = ice * raw_strength[tile, at]
            s1 = ice * raw_stress[0, tile, at]
            s2 = ice * raw_stress[1, tile, at]
            push = (STEP_WEIGHT * DAMP) * ice
            low = firm * (KEEP * 0.125)
            made = {
                U: ext[U, tile, inside],
                V: ext[V, tile, inside],
                A: s1 + s2,
                B: s1 - s2,
                T: (2.0 * ice) * raw_stress[2, tile, at],
                Q: firm * (KEEP * 0.5),
                GX: push * (raw_force[0, tile, at] + DRAG_COEF * raw_force[2, tile, at]),
                GY: push * (raw_force[1, tile, at] + DRAG_COEF * raw_force[3, tile, at]),
            }
            for level in range(count):
                stiff = 3.0 - 2.0 * raw_regime[level, tile, at].astype(jnp.float32)
                made[C + level] = low * stiff
            for field in range(A, fields):
                ext[field, tile, inside] = made[field]
            total = None
            for field, place in places.items():
                moved = spin(made[field], place if tile == 0 else place + widths[field])
                total = moved if total is None else jnp.where(lane >= place, moved, total)
            packs.append(total)
        pack_west[at] = packs[0]
        pack_east[at] = packs[1]
        return 0

    lax.fori_loop(0, groups, prepare, 0, unroll=2)

    pl.semaphore_wait(barrier, greeted)

    def rim_copy(index, src, dst, lat, lon):
        return pltpu.make_async_remote_copy(
            src_ref=src,
            dst_ref=dst,
            send_sem=rim_send.at[index],
            recv_sem=rim_recv.at[index],
            device_id=(lat, lon),
            device_id_type=MESH,
        )

    top, middle, bottom = pl.ds(0, EDGE), pl.ds(EDGE, groups), pl.ds(EDGE + groups, EDGE)
    first, last = pl.ds(0, EDGE), pl.ds(groups - EDGE, EDGE)
    first_inside, last_inside = pl.ds(EDGE, EDGE), pl.ds(groups, EDGE)
    sides = [
        rim_copy(0, pack_west, rim_east.at[middle], me, west),
        rim_copy(1, pack_east, rim_west.at[middle], me, east),
    ]
    ups = [
        rim_copy(2, pack_west.at[first], rim_east.at[bottom], north, west),
        rim_copy(3, pack_east.at[first], rim_west.at[bottom], north, east),
        rim_copy(4, ext.at[:, :, first_inside], ext.at[:, :, bottom], north, here),
    ]
    downs = [
        rim_copy(5, pack_west.at[last], rim_east.at[top], south, west),
        rim_copy(6, pack_east.at[last], rim_west.at[top], south, east),
        rim_copy(7, ext.at[:, :, last_inside], ext.at[:, :, top], south, here),
    ]
    for copy in sides:
        copy.start()

    @pl.when(me > 0)
    def _():
        for copy in ups:
            copy.start()

    @pl.when(me < lats - 1)
    def _():
        for copy in downs:
            copy.start()

    def blank(at):
        nothing = jnp.zeros((EDGE, SUBLANES, LANES), jnp.float32)
        rim_east[at] = nothing
        rim_west[at] = nothing
        for field in range(fields):
            for tile in range(2):
                ext[field, tile, at] = nothing

    @pl.when(me == 0)
    def _():
        blank(top)

    @pl.when(me == lats - 1)
    def _():
        blank(bottom)

    for work in (work_u, work_v, work_a, work_b, work_t):
        for tile in range(3):
            work[tile, pl.ds(0, 8), :] = jnp.zeros((8, LANES), jnp.float32)
            work[tile, pl.ds(span + 8, 8), :] = jnp.zeros((8, LANES), jnp.float32)

    for copy in sides:
        copy.wait_recv()

    @pl.when(me < lats - 1)
    def _():
        for copy in ups:
            copy.wait_recv()

    @pl.when(me > 0)
    def _():
        for copy in downs:
            copy.wait_recv()

    moving = {U: work_u, V: work_v, A: work_a, B: work_b, T: work_t}
    right_end = lane == LANES - 1
    left_end = lane == 0

    def across(tiles):
        ahead = [spin(cells, -1) for cells in tiles]
        behind = [spin(cells, 1) for cells in tiles]
        return [
            jnp.where(right_end, ahead[(t + 1) % 3], ahead[t])
            - jnp.where(left_end, behind[(t + 2) % 3], behind[t])
            for t in range(3)
        ]

    core = lax.rem(me, 2)
    chip = me // 2
    chips = lats // 2
    sign = jnp.where(core == 0, 1, chips - 1)

    def partner(step):
        hop = jnp.where((step == 0) | (step == 4), sign, 0)
        hop = jnp.where((step == 1) | (step == 3), 2, hop)
        hop = jnp.where((step == 2) | (step == 5), chips - sign, hop)
        swap = jnp.where((step == 3) | (step == 4) | (step == 5) | (step == 6), 1, 0)
        return lax.rem(chip + hop, chips) * 2 + lax.rem(core + swap, 2)

    def route_copy(step, lat):
        return pltpu.make_async_remote_copy(
            src_ref=outbox.at[lat],
            dst_ref=blocks.at[me],
            send_sem=route_send.at[step],
            recv_sem=route_recv.at[step],
            device_id=(lat, here),
            device_id_type=MESH,
        )

    def subcycles(target):
        base = order[target] * (block_rows // SUBLANES)

        def wide(field, tile, row):
            return ext[field, tile, base + row // SUBLANES]

        for row in range(0, span, 8):
            from_east = rim_east[base + row // SUBLANES]
            from_west = rim_west[base + row // SUBLANES]
            for field, place in places.items():
                cells = jnp.where(
                    lane < LANES // 2,
                    spin(from_east, -place),
                    spin(from_west, -place - widths[field]),
                )
                if field in moving:
                    moving[field][2, pl.ds(row + 8, 8), :] = cells
                else:
                    edge[field, pl.ds(row, 8), :] = cells
            for field, work in moving.items():
                for tile in range(2):
                    work[tile, pl.ds(row + 8, 8), :] = wide(field, tile, row)

        def fixed(field, tile, row):
            return edge[field, pl.ds(row, 8), :] if tile == 2 else wide(field, tile, row)

        for level in range(count):
            reach = 2 * (count - 1 - level)
            low = (RIM - reach - 1) // 8 * 8
            high = -(-(RIM + block_rows + reach + 1) // 8) * 8
            for row in range(low, high, 8):
                at = pl.ds(row + 8, 8)
                over, under = pl.ds(row + 9, 8), pl.ds(row + 7, 8)
                u_x = across([work_u[t, at, :] for t in range(3)])
                v_x = across([work_v[t, at, :] for t in range(3)])
                for t in range(3):
                    u_y = work_u[t, over, :] - work_u[t, under, :]
                    v_y = work_v[t, over, :] - work_v[t, under, :]
                    c = fixed(C + level, t, row)
                    q = fixed(Q, t, row)
                    both = u_x[t] + v_y
                    work_a[t, at, :] = KEEP * work_a[t, at, :] + (c * (both + 2.0 * u_x[t]) - q)
                    work_b[t, at, :] = KEEP * work_b[t, at, :] + (c * (both + 2.0 * v_y) - q)
                    work_t[t, at, :] = KEEP * work_t[t, at, :] + c * (u_y + v_x[t])
            low = (RIM - reach) // 8 * 8
            high = -(-(RIM + block_rows + reach) // 8) * 8
            final = level == count - 1
            for row in range(low, high, 8):
                at = pl.ds(row + 8, 8)
                over, under = pl.ds(row + 9, 8), pl.ds(row + 7, 8)
                here_a = [work_a[t, at, :] for t in range(3)]
                here_t = [work_t[t, at, :] for t in range(3)]
                a_x = across(here_a)
                t_x = across(here_t)
                for t in range(2 if final else 3):
                    u = work_u[t, at, :]
                    v = work_v[t, at, :]
                    f_x = a_x[t] + (work_t[t, over, :] - work_t[t, under, :])
                    f_y = t_x[t] + (work_b[t, over, :] - work_b[t, under, :])
                    gain = jnp.where(fixed(Q, t, row) > 0.0, DAMP, 0.0)
                    turn = STEP_WEIGHT * CORIOLIS
                    push = STEP_WEIGHT * 0.25
                    next_u = gain * (u + (turn * v + push * f_x)) + fixed(GX, t, row)
                    next_v = gain * (v + (push * f_y - turn * u)) + fixed(GY, t, row)
                    if final:
                        here_b = work_b[t, at, :]
                        done = (
                            next_u,
                            next_v,
                            0.5 * (here_a[t] + here_b),
                            0.5 * (here_a[t] - here_b),
                            0.5 * here_t[t],
                        )
                        lanes = pl.ds(t * LANES, LANES)
                        for part, cells in enumerate(done):
                            outbox[target, part, pl.ds(row - RIM, 8), lanes] = cells
                    else:
                        work_u[t, at, :] = next_u
                        work_v[t, at, :] = next_v

    def deliver(step, _):
        lat = partner(step)
        subcycles(lat)

        @pl.when(step < lats - 1)
        def _():
            route_copy(step, lat).start()

        return 0

    lax.fori_loop(0, lats, deliver, 0)

    own = pltpu.make_async_copy(outbox.at[me], blocks.at[me], own_sem)
    own.start()

    def exchange(j, _):
        taker = route[me, j]
        for part in range(block_rows // 8):
            at = pl.ds(part * 8, 8)
            group = j * (block_rows // SUBLANES) + part
            row = pl.multiple_of(group * SUBLANES, SUBLANES)
            for tile in range(2):
                lanes = pl.ds(tile * LANES, LANES)
                icy = ext[Q, tile, group + EDGE] > 0.0
                for axis in range(2):
                    drift = outbox[taker, axis, at, lanes] - raw_force[2 + axis, tile, group]
                    flux[axis, pl.ds(row, 8), lanes] = jnp.where(icy, DRAG_COEF * drift, 0.0)
        return 0

    lax.fori_loop(0, lats, exchange, 0)

    for copy in sides:
        copy.wait_send()

    @pl.when(me > 0)
    def _():
        for copy in ups:
            copy.wait_send()

    @pl.when(me < lats - 1)
    def _():
        for copy in downs:
            copy.wait_send()

    own.wait()

    def settle(step, _):
        route_copy(step, partner(step)).wait()
        return 0

    lax.fori_loop(0, lats - 1, settle, 0)


def per_device(lats, lons, ice_state, ocean_forcing, ice_strength, ice_mask, yield_mask, ice_route):
    count, rows, columns = yield_mask.shape
    block_rows = rows // lats
    span = block_rows + 2 * RIM
    fields = C + count
    f32 = jnp.float32
    hbm = pl.BlockSpec(memory_space=pl.ANY)
    vmem = pl.BlockSpec(memory_space=pltpu.VMEM)
    work = pltpu.VMEM((3, span + 16, LANES), f32)
    dma = pltpu.SemaphoreType.DMA
    groups = rows // SUBLANES

    def grouped(lead, count, kind=f32):
        return pltpu.VMEM(lead + (count, SUBLANES, LANES), kind)

    def split(cells):
        return cells.reshape(cells.shape[:-2] + (groups, SUBLANES, columns))

    return pl.pallas_call(
        functools.partial(kernel, count, lats, lons),
        out_shape=(
            pltpu.VMEM((2, rows, columns), f32),
            pltpu.VMEM((lats, 5, block_rows, columns), f32),
        ),
        in_specs=[pl.BlockSpec(memory_space=pltpu.SMEM)] + [hbm] * 5,
        out_specs=(vmem, vmem),
        scratch_shapes=[
            grouped((fields, 2), groups + 2 * EDGE),
            grouped((3, 2), groups),
            grouped((4, 2), groups),
            grouped((2,), groups),
            grouped((2,), groups, jnp.int32),
            grouped((count, 2), groups, jnp.int32),
            grouped((), groups),
            grouped((), groups),
            grouped((), groups + 2 * EDGE),
            grouped((), groups + 2 * EDGE),
            work,
            work,
            work,
            work,
            work,
            pltpu.VMEM((fields, span, LANES), f32),
            pltpu.VMEM((lats, 5, block_rows, columns), f32),
            pltpu.SMEM((lats,), jnp.int32),
            dma((12,)),
            dma((8,)),
            dma((8,)),
            dma((lats - 1,)),
            dma((lats - 1,)),
            dma,
        ],
        compiler_params=pltpu.CompilerParams(collective_id=0, has_side_effects=True),
        name="ice_step",
    )(
        ice_route,
        split(ice_state),
        split(ocean_forcing),
        split(ice_strength),
        split(ice_mask),
        split(yield_mask),
    )


def solution(mesh):
    return jax.shard_map(
        functools.partial(per_device, mesh.shape["lat"], mesh.shape["lon"]),
        mesh=mesh,
        in_specs=(
            P(None, "lat", "lon"),
            P(None, "lat", "lon"),
            P("lat", "lon"),
            P("lat", "lon"),
            P(None, "lat", "lon"),
            P(),
        ),
        out_specs=(P(None, "lat", "lon"), P("lat", None, None, "lon")),
        check_vma=False,
    )
```

```python
import functools

import jax
import jax.numpy as jnp
from jax import lax
from jax.experimental import pallas as pl
from jax.experimental.pallas import tpu as pltpu
from jax.sharding import PartitionSpec as P

RELAX_RATE = 1.0
STEP_WEIGHT = 0.5
DRAG_COEF = 0.5
CORIOLIS = 0.3

KEEP = 1.0 / (1.0 + RELAX_RATE)
DAMP = 1.0 / (1.0 + STEP_WEIGHT * DRAG_COEF)

MESH = pl.DeviceIdType.MESH
LANES = 128
HALF = LANES // 2
SUBLANES = 8
RIM = 16
EDGE = RIM // SUBLANES

U, V, A, B, T, Q, GX, GY, C = range(9)
MOVING = 5


def layout(count):
    deep = 2 * count
    widths = {U: deep, V: deep, A: deep - 1, T: deep - 1, Q: deep - 1, C: deep - 1}
    widths.update({B: deep - 2, GX: deep - 2, GY: deep - 2})
    for level in range(1, count):
        widths[C + level] = deep - 1 - 2 * level
    names = list(widths)

    def window(start, width):
        return {(start + i) % LANES for i in range(width)}

    def settle(index, to_west, to_east):
        if index == len(names):
            return {}
        width = widths[names[index]]
        for turn in range(LANES - width + 1):
            mine, other = window(turn, width), window(HALF + turn - width, width)
            if mine & to_west or other & to_east:
                continue
            rest = settle(index + 1, to_west | mine, to_east | other)
            if rest is not None:
                return {names[index]: (turn, (HALF + turn - width) % LANES), **rest}
            if index < len(names) - 3:
                return None
        free_west = [p for p in range(LANES - width + 1) if not window(p, width) & to_west]
        free_east = [p for p in range(LANES - width + 1) if not window(p, width) & to_east]
        if not free_west or not free_east:
            return None
        west, east = free_west[0], free_east[0]
        rest = settle(index + 1, to_west | window(west, width), to_east | window(east, width))
        return None if rest is None else {names[index]: (west, east), **rest}

    return widths, settle(0, set(), set())


def spin(cells, shift):
    shift = shift % LANES
    return cells if shift == 0 else pltpu.roll(cells, shift, 1)


def lay(lane, parts):
    parts = sorted(parts, key=lambda part: part[0])
    start, width, cells = parts[-1]
    total = cells if start + width > LANES else parts[0][2]
    for start, width, cells in parts:
        total = jnp.where(lane >= start, cells, total)
    return total


def stress(u_x, u_y, v_x, v_y, a, b, t, c, q):
    both = u_x + v_y
    next_a = KEEP * a + (c * (both + 2.0 * u_x) - q)
    next_b = KEEP * b + (c * (both + 2.0 * v_y) - q)
    return next_a, next_b, KEEP * t + c * (u_y + v_x)


def momentum(u, v, f_x, f_y, q, g_x, g_y):
    gain = jnp.where(q > 0.0, DAMP, 0.0)
    turn, push = STEP_WEIGHT * CORIOLIS, STEP_WEIGHT * 0.25
    next_u = gain * (u + (turn * v + push * f_x)) + g_x
    next_v = gain * (v + (push * f_y - turn * u)) + g_y
    return next_u, next_v


def finish(u, v, a, b, t):
    return u, v, 0.5 * (a + b), 0.5 * (a - b), 0.5 * t


def reaches(count, level, rows):
    reach = 2 * (count - 1 - level)

    def span(extra):
        low = (RIM - reach - extra) // SUBLANES
        high = -(-(RIM + rows + reach + extra) // SUBLANES)
        return range(low, high)

    return span(1), span(0)


def kernel(
    count,
    lats,
    lons,
    route_in,
    state,
    forcing,
    strength,
    mask,
    regime,
    flux,
    blocks,
    raw_state,
    raw_force,
    raw_strength,
    raw_mask,
    raw_regime,
    ext,
    pack_west,
    pack_east,
    rim_east,
    rim_west,
    work_u,
    work_v,
    work_a,
    work_b,
    work_t,
    side_u,
    side_v,
    side_a,
    side_b,
    side_t,
    side_fixed,
    sides,
    outbox,
    side_out,
    side_in,
    route,
    order,
    load_sem,
    rim_send,
    rim_recv,
    route_send,
    route_recv,
    side_send,
    side_recv,
    own_sem,
    ready,
):
    fields = C + count
    widths, places = layout(count)
    groups = state.shape[1]
    rows = groups * SUBLANES
    block_rows = rows // lats
    block_groups = block_rows // SUBLANES
    deep = 2 * count
    me = lax.axis_index("lat")
    here = lax.axis_index("lon")
    west = lax.rem(here + lons - 1, lons)
    east = lax.rem(here + 1, lons)
    north = lax.rem(me + lats - 1, lats)
    south = lax.rem(me + 1, lats)
    odd = lax.rem(here, 2)

    barrier = pltpu.get_barrier_semaphore()
    for step in range(1, lats):
        pl.semaphore_signal(
            barrier, inc=1, device_id=(lax.rem(me + step, lats), here), device_id_type=MESH
        )
    around = [(lat, lon) for lon in (west, east) for lat in (north, me, south)]

    loads = []

    def load(src, dst):
        copy = pltpu.make_async_copy(src, dst, load_sem.at[len(loads)])
        copy.start()
        loads.append(copy)

    def load_groups(at):
        first = len(loads)
        load(state.at[:, at], raw_state.at[:, at])
        load(forcing.at[:, at], raw_force.at[:, at])
        load(strength.at[at], raw_strength.at[at])
        load(mask.at[at], raw_mask.at[at])
        load(regime.at[:, at], raw_regime.at[:, at])
        return loads[first:]

    half = (groups - 2 * EDGE) // 2
    chunks = [
        load_groups(pl.ds(0, EDGE)),
        load_groups(pl.ds(groups - EDGE, EDGE)),
        load_groups(pl.ds(EDGE, half)),
        load_groups(pl.ds(EDGE + half, groups - 2 * EDGE - half)),
    ]
    load(route_in, route)

    lane = lax.broadcasted_iota(jnp.int32, (SUBLANES, LANES), 1)
    right_part = (lane >= HALF // 2) & (lane < HALF)

    def fold(left, right):
        return jnp.where(right_part, spin(right, HALF), left)

    side_moving = (side_u, side_v, side_a, side_b, side_t)

    def side_rows(group):
        row = (group + 1) * SUBLANES
        return pl.ds(row if isinstance(group, int) else pl.multiple_of(row, SUBLANES), SUBLANES)

    def put_side(field, group, cells):
        if field < MOVING:
            side_moving[field][side_rows(group), :] = cells
        else:
            side_fixed[field - MOVING, group] = cells

    def get_side(field, group):
        if field < MOVING:
            return side_moving[field][side_rows(group), :]
        return side_fixed[field - MOVING, group]

    def prepare(at, _):
        made = []
        for tile in range(2):
            lanes = pl.ds(tile * LANES, LANES)
            ice = raw_mask[at, :, lanes].astype(jnp.float32)
            firm = ice * raw_strength[at, :, lanes]
            s1 = ice * raw_state[2, at, :, lanes]
            s2 = ice * raw_state[3, at, :, lanes]
            push = (STEP_WEIGHT * DAMP) * ice
            low = firm * (KEEP * 0.125)
            cells = {
                U: raw_state[0, at, :, lanes],
                V: raw_state[1, at, :, lanes],
                A: s1 + s2,
                B: s1 - s2,
                T: (2.0 * ice) * raw_state[4, at, :, lanes],
                Q: firm * (KEEP * 0.5),
                GX: push * (raw_force[0, at, :, lanes] + DRAG_COEF * raw_force[2, at, :, lanes]),
                GY: push * (raw_force[1, at, :, lanes] + DRAG_COEF * raw_force[3, at, :, lanes]),
            }
            for level in range(count):
                stiff = 3.0 - 2.0 * raw_regime[level, at, :, lanes].astype(jnp.float32)
                cells[C + level] = low * stiff
            for field in range(fields):
                ext[field, tile, at + EDGE] = cells[field]
            made.append(cells)
        to_west, to_east = [], []
        for field, (start, other) in places.items():
            width = widths[field]
            both = fold(made[0][field], made[1][field])
            put_side(field, at + EDGE, both)
            moved = spin(both, start)
            to_west.append((start, width, moved))
            if other != (HALF + start - width) % LANES:
                moved = spin(both, other + width - HALF)
            to_east.append((other, width, moved))
        pack_west[at] = lay(lane, to_west)
        pack_east[at] = lay(lane, to_east)
        return 0

    def copies_done(chunk):
        for copy in chunk:
            copy.wait()

    copies_done(chunks[0] + chunks[1])
    for end in (0, groups - EDGE):
        for group in range(EDGE):
            prepare(end + group, 0)

    def rim_copy(index, src, dst, lat, lon):
        return pltpu.make_async_remote_copy(
            src_ref=src,
            dst_ref=dst,
            send_sem=rim_send.at[index],
            recv_sem=rim_recv.at[index],
            device_id=(lat, lon),
            device_id_type=MESH,
        )

    far = C + sum(1 for level in range(count) if deep - 1 - 2 * level > SUBLANES)
    near_count = fields - far
    top, middle, bottom = pl.ds(0, EDGE), pl.ds(EDGE, groups), pl.ds(EDGE + groups, EDGE)
    first, last = pl.ds(0, EDGE), pl.ds(groups - EDGE, EDGE)
    wide_fields, late_fields = pl.ds(0, far), pl.ds(far, near_count)

    def lat_copy(index, part, src, dst, lat):
        return rim_copy(index, ext.at[part, :, src], ext.at[part, :, dst], lat, here)

    lat_ups = [
        lat_copy(0, wide_fields, pl.ds(EDGE, EDGE), bottom, north),
        lat_copy(1, late_fields, pl.ds(EDGE, 1), pl.ds(EDGE + groups, 1), north),
    ]
    lat_downs = [
        lat_copy(2, wide_fields, pl.ds(groups, EDGE), top, south),
        lat_copy(3, late_fields, pl.ds(groups + EDGE - 1, 1), pl.ds(EDGE - 1, 1), south),
    ]
    lon_both = [
        rim_copy(4, pack_west, rim_east.at[middle], me, west),
        rim_copy(5, pack_east, rim_west.at[middle], me, east),
    ]
    lon_ups = [
        rim_copy(6, pack_west.at[first], rim_east.at[bottom], north, west),
        rim_copy(7, pack_east.at[first], rim_west.at[bottom], north, east),
    ]
    lon_downs = [
        rim_copy(8, pack_west.at[last], rim_east.at[top], south, west),
        rim_copy(9, pack_east.at[last], rim_west.at[top], south, east),
    ]
    has_north, has_south = me > 0, me < lats - 1

    @pl.when(odd == 0)
    def _():
        pl.semaphore_wait(barrier, lats - 1)

    @pl.when(odd == 1)
    def _():
        pl.semaphore_wait(barrier, lats - 1 + len(around))

    @pl.when(has_north)
    def _():
        for copy in lat_ups:
            copy.start()

    @pl.when(has_south)
    def _():
        for copy in lat_downs:
            copy.start()

    @pl.when(odd == 0)
    def _():
        for target in around:
            pl.semaphore_signal(barrier, inc=1, device_id=target, device_id_type=MESH)

    @pl.when(odd == 1)
    def _():
        for target in around:
            pl.semaphore_signal(ready, inc=1, device_id=target, device_id_type=MESH)

    copies_done(chunks[2])
    lax.fori_loop(EDGE, EDGE + half, prepare, 0, unroll=7)
    copies_done(chunks[3])
    lax.fori_loop(EDGE + half, groups - EDGE, prepare, 0, unroll=7)

    @pl.when(odd == 0)
    def _():
        pl.semaphore_wait(ready, len(around))

    for copy in lon_both:
        copy.start()

    @pl.when(has_north)
    def _():
        for copy in lon_ups:
            copy.start()

    @pl.when(has_south)
    def _():
        for copy in lon_downs:
            copy.start()

    loads[-1].wait()
    for lat in range(lats):
        block = jnp.int32(0)
        for j in range(1, lats):
            apart = route[me, j] - lat
            block = block + j * (1 - lax.div(apart * apart + 63, 64))
        order[lat] = lax.rem(block, lats)

    def blank(at):
        nothing = jnp.zeros((EDGE, SUBLANES, LANES), jnp.float32)
        rim_east[at] = nothing
        rim_west[at] = nothing
        for field in range(fields):
            for tile in range(2):
                ext[field, tile, at] = nothing

    @pl.when(me == 0)
    def _():
        blank(top)

    @pl.when(me == lats - 1)
    def _():
        blank(bottom)

    line = jnp.zeros((SUBLANES, LANES), jnp.float32)
    for work in (work_u, work_v, work_a, work_b, work_t):
        for tile in range(2):
            work[tile, pl.ds(0, SUBLANES), :] = line
            work[tile, pl.ds(block_rows + 2 * RIM + SUBLANES, SUBLANES), :] = line
    for side in (side_u, side_v, side_a, side_b, side_t):
        side[pl.ds(0, SUBLANES), :] = line
        side[pl.ds(rows + 2 * RIM + SUBLANES, SUBLANES), :] = line

    @pl.when(has_south)
    def _():
        for copy in lat_ups:
            copy.wait_recv()

    @pl.when(has_north)
    def _():
        for copy in lat_downs:
            copy.wait_recv()

    core = lax.rem(me, 2)
    chip = me // 2
    chips = lats // 2

    def hop_of(step, core):
        sign = jnp.where(core == 0, 1, chips - 1)
        hop = jnp.where((step == 0) | (step == 4), sign, 0)
        hop = jnp.where((step == 1) | (step == 3), 2, hop)
        return jnp.where((step == 2) | (step == 5), chips - sign, hop)

    def swap_of(step):
        return jnp.where((step >= 3) & (step <= 6), 1, 0)

    def taker_of(step):
        lat_chip = lax.rem(chip + hop_of(step, core), chips)
        return lat_chip * 2 + lax.rem(core + swap_of(step), 2)

    def giver_of(step):
        other = lax.rem(core + swap_of(step), 2)
        return lax.rem(chip + chips - hop_of(step, other), chips) * 2 + other

    def route_copy(step, lat, slot):
        return pltpu.make_async_remote_copy(
            src_ref=outbox.at[lat],
            dst_ref=blocks.at[slot],
            send_sem=route_send.at[step],
            recv_sem=route_recv.at[step],
            device_id=(lat, here),
            device_id_type=MESH,
        )

    def side_copy(step, lat, slot):
        return pltpu.make_async_remote_copy(
            src_ref=side_out.at[lat],
            dst_ref=side_in.at[slot],
            send_sem=side_send.at[step],
            recv_sem=side_recv.at[step],
            device_id=(lat, here),
            device_id_type=MESH,
        )

    right_end = lane == LANES - 1
    left_end = lane == 0

    def across(tiles):
        ahead = [spin(cells, -1) for cells in tiles]
        behind = [spin(cells, 1) for cells in tiles]
        return [
            jnp.where(right_end, ahead[1 - t], ahead[t])
            - jnp.where(left_end, behind[1 - t], behind[t])
            for t in range(2)
        ]

    def around_row(group):
        row = (group + 1) * SUBLANES
        return [pl.ds(row + shift, SUBLANES) for shift in (0, 1, -1)]

    def subcycles(target):
        base = order[target] * block_groups

        def fixed(field, tile, group):
            return ext[field, tile, base + group]

        for group in range(block_groups + 2 * EDGE):
            at = around_row(group)[0]
            for tile in range(2):
                work_u[tile, at, :] = fixed(U, tile, group)
                work_v[tile, at, :] = fixed(V, tile, group)

        for level in range(count):
            stress_span, momentum_span = reaches(count, level, block_rows)
            for group in stress_span:
                at, over, under = around_row(group)
                u_x = across([work_u[t, at, :] for t in range(2)])
                v_x = across([work_v[t, at, :] for t in range(2)])
                for t in range(2):
                    u_y = work_u[t, over, :] - work_u[t, under, :]
                    v_y = work_v[t, over, :] - work_v[t, under, :]
                    if level == 0:
                        old = [fixed(field, t, group) for field in (A, B, T)]
                    else:
                        old = [work[t, at, :] for work in (work_a, work_b, work_t)]
                    c, q = fixed(C + level, t, group), fixed(Q, t, group)
                    new = stress(u_x[t], u_y, v_x[t], v_y, *old, c, q)
                    for work, cells in zip((work_a, work_b, work_t), new):
                        work[t, at, :] = cells
            final = level == count - 1
            for group in momentum_span:
                at, over, under = around_row(group)
                here_a = [work_a[t, at, :] for t in range(2)]
                here_t = [work_t[t, at, :] for t in range(2)]
                a_x, t_x = across(here_a), across(here_t)
                for t in range(2):
                    f_x = a_x[t] + (work_t[t, over, :] - work_t[t, under, :])
                    f_y = t_x[t] + (work_b[t, over, :] - work_b[t, under, :])
                    new = momentum(
                        work_u[t, at, :],
                        work_v[t, at, :],
                        f_x,
                        f_y,
                        fixed(Q, t, group),
                        fixed(GX, t, group),
                        fixed(GY, t, group),
                    )
                    if final:
                        done = finish(*new, here_a[t], work_b[t, at, :], here_t[t])
                        inside = pl.ds((group - EDGE) * SUBLANES, SUBLANES)
                        for part, cells in enumerate(done):
                            outbox[target, part, inside, pl.ds(t * LANES, LANES)] = cells
                    else:
                        work_u[t, at, :], work_v[t, at, :] = new

    def deliver(step, _):
        lat = taker_of(step)
        subcycles(lat)

        @pl.when(step < lats - 1)
        def _():
            route_copy(step, lat, me).start()

        return 0

    lax.fori_loop(0, lats - 2, deliver, 0)

    for copy in lon_both:
        copy.wait_recv()

    @pl.when(has_south)
    def _():
        for copy in lon_ups:
            copy.wait_recv()

    @pl.when(has_north)
    def _():
        for copy in lon_downs:
            copy.wait_recv()

    def unpack(group, names, beyond):
        from_east, from_west = rim_east[group], rim_west[group]
        for field in names:
            start, other = places[field]
            width = widths[field]
            if other == (HALF + start - width) % LANES:
                end = (start + HALF // 2) % LANES
                if start < end:
                    mine = (lane >= start) & (lane < end)
                else:
                    mine = (lane >= start) | (lane < end)
                rim = spin(jnp.where(mine, from_east, from_west), HALF - start)
            else:
                rim = jnp.where(
                    lane < LANES - HALF // 2,
                    spin(from_east, HALF - start),
                    spin(from_west, -other - width),
                )
            if beyond:
                base = fold(ext[field, 0, group], ext[field, 1, group])
            else:
                base = get_side(field, group)
            put_side(field, group, jnp.where(lane < HALF, base, rim))

    for group in (0, groups + 2 * EDGE - 1):
        unpack(group, range(far), True)
    for group in (1, groups + 2 * EDGE - 2):
        unpack(group, range(fields), True)

    def unpack_inside(group, _):
        unpack(group, range(fields), False)
        return 0

    lax.fori_loop(EDGE, groups + EDGE, unpack_inside, 0, unroll=8)

    def beside(cells):
        return spin(cells, -1) - spin(cells, 1)

    def middle_of(part):
        return 2 * deep * part + deep

    for level in range(count):
        stress_span, momentum_span = reaches(count, level, rows)
        for group in stress_span:
            at, over, under = around_row(group)
            new = stress(
                beside(side_u[at, :]),
                side_u[over, :] - side_u[under, :],
                beside(side_v[at, :]),
                side_v[over, :] - side_v[under, :],
                side_a[at, :],
                side_b[at, :],
                side_t[at, :],
                side_fixed[C + level - MOVING, group],
                side_fixed[Q - MOVING, group],
            )
            side_a[at, :], side_b[at, :], side_t[at, :] = new
        for group in momentum_span:
            at, over, under = around_row(group)
            a, b, t = side_a[at, :], side_b[at, :], side_t[at, :]
            new = momentum(
                side_u[at, :],
                side_v[at, :],
                beside(a) + (side_t[over, :] - side_t[under, :]),
                beside(t) + (side_b[over, :] - side_b[under, :]),
                side_fixed[Q - MOVING, group],
                side_fixed[GX - MOVING, group],
                side_fixed[GY - MOVING, group],
            )
            if level < count - 1:
                side_u[at, :], side_v[at, :] = new
            else:
                parts = []
                for part, cells in enumerate(finish(*new, a, b, t)):
                    cells = jnp.where(lane < HALF // 2, cells, spin(cells, HALF))
                    start = middle_of(part) - deep
                    parts.append((start, 2 * deep, spin(cells, middle_of(part))))
                sides[group - EDGE] = lay(lane, parts)

    def deliver_sides(step, _):
        lat = taker_of(step)
        base = order[lat] * block_groups
        for group in range(block_groups):
            side_out[lat, group] = sides[base + group]

        @pl.when(step < lats - 1)
        def _():
            side_copy(step, lat, me).start()

        return 0

    lax.fori_loop(0, lats, deliver_sides, 0)
    lax.fori_loop(lats - 2, lats, deliver, 0)

    own = pltpu.make_async_copy(outbox.at[me], blocks.at[me], own_sem)
    own.start()

    def place(packed, part, tiles):
        moved = spin(packed, -middle_of(part))
        return (
            jnp.where(lane < deep, moved, tiles[0]),
            jnp.where(lane >= LANES - deep, moved, tiles[1]),
        )

    both_lanes = [pl.ds(tile * LANES, LANES) for tile in range(2)]

    def exchange(j, _):
        taker = route[me, j]
        for part in range(block_groups):
            at = pl.ds(part * SUBLANES, SUBLANES)
            group = j * block_groups + part
            row = pl.multiple_of(group * SUBLANES, SUBLANES)
            for axis in range(2):
                drift = [outbox[taker, axis, at, lanes] for lanes in both_lanes]
                drift = place(sides[group], axis, drift)
                for tile, lanes in enumerate(both_lanes):
                    icy = ext[Q, tile, group + EDGE] > 0.0
                    moved = drift[tile] - raw_force[2 + axis, group, :, lanes]
                    flux[axis, pl.ds(row, SUBLANES), lanes] = jnp.where(icy, DRAG_COEF * moved, 0.0)
        return 0

    lax.fori_loop(0, lats, exchange, 0)

    def mend(slot, source):
        for group in range(block_groups):
            packed = source[slot, group]
            at = pl.ds(group * SUBLANES, SUBLANES)
            for part in range(MOVING):
                tiles = place(packed, part, [blocks[slot, part, at, lanes] for lanes in both_lanes])
                for lanes, cells in zip(both_lanes, tiles):
                    blocks[slot, part, at, lanes] = cells

    own.wait()
    mend(me, side_out)

    def receive(step, _):
        lat = giver_of(step)
        route_copy(step, lat, lat).wait_recv()
        side_copy(step, lat, lat).wait_recv()
        mend(lat, side_in)
        return 0

    lax.fori_loop(0, lats - 1, receive, 0)

    def settle(step, _):
        route_copy(step, taker_of(step), me).wait_send()
        side_copy(step, taker_of(step), me).wait_send()
        return 0

    lax.fori_loop(0, lats - 1, settle, 0)

    for copy in lon_both:
        copy.wait_send()

    @pl.when(has_north)
    def _():
        for copy in lat_ups + lon_ups:
            copy.wait_send()

    @pl.when(has_south)
    def _():
        for copy in lat_downs + lon_downs:
            copy.wait_send()


def per_device(lats, lons, ice_state, ocean_forcing, ice_strength, ice_mask, yield_mask, ice_route):
    count, rows, columns = yield_mask.shape
    block_rows = rows // lats
    fields = C + count
    groups = rows // SUBLANES
    f32, i32 = jnp.float32, jnp.int32
    hbm = pl.BlockSpec(memory_space=pl.ANY)
    vmem = pl.BlockSpec(memory_space=pltpu.VMEM)
    dma = pltpu.SemaphoreType.DMA

    def tiles(*lead, kind=f32, wide=LANES):
        return pltpu.VMEM(lead + (SUBLANES, wide), kind)

    def split(cells):
        return cells.reshape(cells.shape[:-2] + (groups, SUBLANES, columns))

    work = pltpu.VMEM((2, block_rows + 2 * RIM + 2 * SUBLANES, LANES), f32)
    side = pltpu.VMEM((rows + 2 * RIM + 2 * SUBLANES, LANES), f32)
    return pl.pallas_call(
        functools.partial(kernel, count, lats, lons),
        out_shape=(
            pltpu.VMEM((2, rows, columns), f32),
            pltpu.VMEM((lats, 5, block_rows, columns), f32),
        ),
        in_specs=[hbm] * 6,
        out_specs=(vmem, vmem),
        scratch_shapes=[
            tiles(5, groups, wide=columns),
            tiles(4, groups, wide=columns),
            tiles(groups, wide=columns),
            tiles(groups, kind=i32, wide=columns),
            tiles(count, groups, kind=i32, wide=columns),
            tiles(fields, 2, groups + 2 * EDGE),
            tiles(groups),
            tiles(groups),
            tiles(groups + 2 * EDGE),
            tiles(groups + 2 * EDGE),
            work,
            work,
            work,
            work,
            work,
            side,
            side,
            side,
            side,
            side,
            tiles(fields - MOVING, groups + 2 * EDGE),
            tiles(groups),
            pltpu.VMEM((lats, 5, block_rows, columns), f32),
            tiles(lats, block_rows // SUBLANES),
            tiles(lats, block_rows // SUBLANES),
            pltpu.SMEM((lats, lats), i32),
            pltpu.SMEM((lats,), i32),
            dma((21,)),
            dma((10,)),
            dma((10,)),
            dma((lats - 1,)),
            dma((lats - 1,)),
            dma((lats - 1,)),
            dma((lats - 1,)),
            dma,
            pltpu.SemaphoreType.REGULAR,
        ],
        compiler_params=pltpu.CompilerParams(collective_id=0, has_side_effects=True),
        name="ice_step",
    )(
        ice_route,
        split(ice_state),
        split(ocean_forcing),
        split(ice_strength),
        split(ice_mask),
        split(yield_mask),
    )


def solution(mesh):
    return jax.shard_map(
        functools.partial(per_device, mesh.shape["lat"], mesh.shape["lon"]),
        mesh=mesh,
        in_specs=(
            P(None, "lat", "lon"),
            P(None, "lat", "lon"),
            P("lat", "lon"),
            P("lat", "lon"),
            P(None, "lat", "lon"),
            P(),
        ),
        out_specs=(P(None, "lat", "lon"), P("lat", None, None, "lon")),
        check_vma=False,
    )
```

```python
import functools

import jax
import jax.numpy as jnp
from jax import lax
from jax.experimental import pallas as pl
from jax.experimental.pallas import tpu as pltpu
from jax.sharding import PartitionSpec as P

RELAX_RATE = 1.0
STEP_WEIGHT = 0.5
DRAG_COEF = 0.5
CORIOLIS = 0.3

KEEP = 1.0 / (1.0 + RELAX_RATE)
DAMP = 1.0 / (1.0 + STEP_WEIGHT * DRAG_COEF)

MESH = pl.DeviceIdType.MESH
LANES = 128
HALF = LANES // 2
SUBLANES = 8
RIM = 16
EDGE = RIM // SUBLANES

U, V, A, B, T, Q, GX, GY, C = range(9)
MOVING = 5


def layout(count):
    deep = 2 * count
    widths = {U: deep, V: deep, A: deep - 1, T: deep - 1, Q: deep - 1, C: deep - 1}
    widths.update({B: deep - 2, GX: deep - 2, GY: deep - 2})
    for level in range(1, count):
        widths[C + level] = deep - 1 - 2 * level
    names = list(widths)

    def window(start, width):
        return {(start + i) % LANES for i in range(width)}

    def settle(index, to_west, to_east):
        if index == len(names):
            return {}
        width = widths[names[index]]
        for turn in range(LANES - width + 1):
            mine, other = window(turn, width), window(HALF + turn - width, width)
            if mine & to_west or other & to_east:
                continue
            rest = settle(index + 1, to_west | mine, to_east | other)
            if rest is not None:
                return {names[index]: (turn, (HALF + turn - width) % LANES), **rest}
            if index < len(names) - 3:
                return None
        free_west = [p for p in range(LANES - width + 1) if not window(p, width) & to_west]
        free_east = [p for p in range(LANES - width + 1) if not window(p, width) & to_east]
        if not free_west or not free_east:
            return None
        west, east = free_west[0], free_east[0]
        rest = settle(index + 1, to_west | window(west, width), to_east | window(east, width))
        return None if rest is None else {names[index]: (west, east), **rest}

    return widths, settle(0, set(), set())


def spin(cells, shift):
    shift = shift % LANES
    return cells if shift == 0 else pltpu.roll(cells, shift, 1)


def lay(lane, parts):
    parts = sorted(parts, key=lambda part: part[0])
    start, width, cells = parts[-1]
    total = cells if start + width > LANES else parts[0][2]
    for start, width, cells in parts:
        total = jnp.where(lane >= start, cells, total)
    return total


def stress(u_x, u_y, v_x, v_y, a, b, t, c, q):
    both = u_x + v_y
    next_a = KEEP * a + (c * (both + 2.0 * u_x) - q)
    next_b = KEEP * b + (c * (both + 2.0 * v_y) - q)
    return next_a, next_b, KEEP * t + c * (u_y + v_x)


def momentum(u, v, f_x, f_y, q, g_x, g_y):
    gain = jnp.where(q > 0.0, DAMP, 0.0)
    turn, push = STEP_WEIGHT * CORIOLIS, STEP_WEIGHT * 0.25
    next_u = gain * (u + (turn * v + push * f_x)) + g_x
    next_v = gain * (v + (push * f_y - turn * u)) + g_y
    return next_u, next_v


def finish(u, v, a, b, t):
    return u, v, 0.5 * (a + b), 0.5 * (a - b), 0.5 * t


def reaches(count, level, rows):
    reach = 2 * (count - 1 - level)

    def span(extra):
        low = (RIM - reach - extra) // SUBLANES
        high = -(-(RIM + rows + reach + extra) // SUBLANES)
        return range(low, high)

    return span(1), span(0)


def kernel(
    count,
    lats,
    lons,
    route_in,
    state,
    forcing,
    strength,
    mask,
    regime,
    flux,
    blocks,
    raw_state,
    raw_force,
    raw_strength,
    raw_mask,
    raw_regime,
    ext,
    pack_west,
    pack_east,
    rim_east,
    rim_west,
    work_u,
    work_v,
    work_a,
    work_b,
    work_t,
    side_u,
    side_v,
    side_a,
    side_b,
    side_t,
    side_fixed,
    sides,
    outbox,
    side_out,
    side_in,
    route,
    order,
    load_sem,
    rim_send,
    rim_recv,
    route_send,
    route_recv,
    side_send,
    side_recv,
    own_sem,
    ready,
):
    fields = C + count
    widths, places = layout(count)
    groups = state.shape[1]
    rows = groups * SUBLANES
    block_rows = rows // lats
    block_groups = block_rows // SUBLANES
    deep = 2 * count
    me = lax.axis_index("lat")
    here = lax.axis_index("lon")
    west = lax.rem(here + lons - 1, lons)
    east = lax.rem(here + 1, lons)
    north = lax.rem(me + lats - 1, lats)
    south = lax.rem(me + 1, lats)
    odd = lax.rem(here, 2)

    barrier = pltpu.get_barrier_semaphore()
    for step in range(1, lats):
        pl.semaphore_signal(
            barrier, inc=1, device_id=(lax.rem(me + step, lats), here), device_id_type=MESH
        )
    around = [(lat, lon) for lon in (west, east) for lat in (north, me, south)]

    loads = []

    def load(src, dst):
        copy = pltpu.make_async_copy(src, dst, load_sem.at[len(loads)])
        copy.start()
        loads.append(copy)

    def load_groups(at):
        first = len(loads)
        load(state.at[:, at], raw_state.at[:, at])
        load(forcing.at[:, at], raw_force.at[:, at])
        load(strength.at[at], raw_strength.at[at])
        load(mask.at[at], raw_mask.at[at])
        load(regime.at[:, at], raw_regime.at[:, at])
        return loads[first:]

    half = (groups - 2 * EDGE) // 2
    chunks = [
        load_groups(pl.ds(0, EDGE)),
        load_groups(pl.ds(groups - EDGE, EDGE)),
        load_groups(pl.ds(EDGE, half)),
        load_groups(pl.ds(EDGE + half, groups - 2 * EDGE - half)),
    ]
    load(route_in, route)

    lane = lax.broadcasted_iota(jnp.int32, (SUBLANES, LANES), 1)
    right_part = (lane >= HALF // 2) & (lane < HALF)

    def fold(left, right):
        return jnp.where(right_part, spin(right, HALF), left)

    side_moving = (side_u, side_v, side_a, side_b, side_t)

    def side_rows(group):
        row = (group + 1) * SUBLANES
        return pl.ds(row if isinstance(group, int) else pl.multiple_of(row, SUBLANES), SUBLANES)

    def put_side(field, group, cells):
        if field < MOVING:
            side_moving[field][side_rows(group), :] = cells
        else:
            side_fixed[field - MOVING, group] = cells

    def get_side(field, group):
        if field < MOVING:
            return side_moving[field][side_rows(group), :]
        return side_fixed[field - MOVING, group]

    def prepare(at, _):
        made = []
        for tile in range(2):
            lanes = pl.ds(tile * LANES, LANES)
            ice = raw_mask[at, :, lanes].astype(jnp.float32)
            firm = ice * raw_strength[at, :, lanes]
            s1 = ice * raw_state[2, at, :, lanes]
            s2 = ice * raw_state[3, at, :, lanes]
            push = (STEP_WEIGHT * DAMP) * ice
            low = firm * (KEEP * 0.125)
            cells = {
                U: raw_state[0, at, :, lanes],
                V: raw_state[1, at, :, lanes],
                A: s1 + s2,
                B: s1 - s2,
                T: (2.0 * ice) * raw_state[4, at, :, lanes],
                Q: firm * (KEEP * 0.5),
                GX: push * (raw_force[0, at, :, lanes] + DRAG_COEF * raw_force[2, at, :, lanes]),
                GY: push * (raw_force[1, at, :, lanes] + DRAG_COEF * raw_force[3, at, :, lanes]),
            }
            for level in range(count):
                stiff = 3.0 - 2.0 * raw_regime[level, at, :, lanes].astype(jnp.float32)
                cells[C + level] = low * stiff
            for field in range(fields):
                ext[field, tile, at + EDGE] = cells[field]
            made.append(cells)
        to_west, to_east = [], []
        for field, (start, other) in places.items():
            width = widths[field]
            both = fold(made[0][field], made[1][field])
            put_side(field, at + EDGE, both)
            moved = spin(both, start)
            to_west.append((start, width, moved))
            if other != (HALF + start - width) % LANES:
                moved = spin(both, other + width - HALF)
            to_east.append((other, width, moved))
        pack_west[at] = lay(lane, to_west)
        pack_east[at] = lay(lane, to_east)
        return 0

    def copies_done(chunk):
        for copy in chunk:
            copy.wait()

    copies_done(chunks[0] + chunks[1])
    for end in (0, groups - EDGE):
        for group in range(EDGE):
            prepare(end + group, 0)

    def rim_copy(index, src, dst, lat, lon):
        return pltpu.make_async_remote_copy(
            src_ref=src,
            dst_ref=dst,
            send_sem=rim_send.at[index],
            recv_sem=rim_recv.at[index],
            device_id=(lat, lon),
            device_id_type=MESH,
        )

    far = C + sum(1 for level in range(count) if deep - 1 - 2 * level > SUBLANES)
    near_count = fields - far
    top, middle, bottom = pl.ds(0, EDGE), pl.ds(EDGE, groups), pl.ds(EDGE + groups, EDGE)
    first, last = pl.ds(0, EDGE), pl.ds(groups - EDGE, EDGE)
    wide_fields, late_fields = pl.ds(0, far), pl.ds(far, near_count)

    def lat_copy(index, part, src, dst, lat):
        return rim_copy(index, ext.at[part, :, src], ext.at[part, :, dst], lat, here)

    lat_ups = [
        lat_copy(0, wide_fields, pl.ds(EDGE, EDGE), bottom, north),
        lat_copy(1, late_fields, pl.ds(EDGE, 1), pl.ds(EDGE + groups, 1), north),
    ]
    lat_downs = [
        lat_copy(2, wide_fields, pl.ds(groups, EDGE), top, south),
        lat_copy(3, late_fields, pl.ds(groups + EDGE - 1, 1), pl.ds(EDGE - 1, 1), south),
    ]
    lon_both = [
        rim_copy(4, pack_west, rim_east.at[middle], me, west),
        rim_copy(5, pack_east, rim_west.at[middle], me, east),
    ]
    lon_ups = [
        rim_copy(6, pack_west.at[first], rim_east.at[bottom], north, west),
        rim_copy(7, pack_east.at[first], rim_west.at[bottom], north, east),
    ]
    lon_downs = [
        rim_copy(8, pack_west.at[last], rim_east.at[top], south, west),
        rim_copy(9, pack_east.at[last], rim_west.at[top], south, east),
    ]
    has_north, has_south = me > 0, me < lats - 1

    @pl.when(odd == 0)
    def _():
        pl.semaphore_wait(barrier, lats - 1)

    @pl.when(odd == 1)
    def _():
        pl.semaphore_wait(barrier, lats - 1 + len(around))

    @pl.when(has_north)
    def _():
        for copy in lat_ups:
            copy.start()

    @pl.when(has_south)
    def _():
        for copy in lat_downs:
            copy.start()

    @pl.when(odd == 0)
    def _():
        for target in around:
            pl.semaphore_signal(barrier, inc=1, device_id=target, device_id_type=MESH)

    @pl.when(odd == 1)
    def _():
        for target in around:
            pl.semaphore_signal(ready, inc=1, device_id=target, device_id_type=MESH)

    copies_done(chunks[2])
    lax.fori_loop(EDGE, EDGE + half, prepare, 0, unroll=7)
    copies_done(chunks[3])
    lax.fori_loop(EDGE + half, groups - EDGE, prepare, 0, unroll=7)

    @pl.when(odd == 0)
    def _():
        pl.semaphore_wait(ready, len(around))

    for copy in lon_both:
        copy.start()

    @pl.when(has_north)
    def _():
        for copy in lon_ups:
            copy.start()

    @pl.when(has_south)
    def _():
        for copy in lon_downs:
            copy.start()

    loads[-1].wait()
    for lat in range(lats):
        block = jnp.int32(0)
        for j in range(1, lats):
            apart = route[me, j] - lat
            block = block + j * (1 - lax.div(apart * apart + 63, 64))
        order[lat] = lax.rem(block, lats)

    def blank(at):
        nothing = jnp.zeros((EDGE, SUBLANES, LANES), jnp.float32)
        rim_east[at] = nothing
        rim_west[at] = nothing
        for field in range(fields):
            for tile in range(2):
                ext[field, tile, at] = nothing

    @pl.when(me == 0)
    def _():
        blank(top)

    @pl.when(me == lats - 1)
    def _():
        blank(bottom)

    line = jnp.zeros((SUBLANES, LANES), jnp.float32)
    for work in (work_u, work_v, work_a, work_b, work_t):
        for tile in range(2):
            work[tile, pl.ds(0, SUBLANES), :] = line
            work[tile, pl.ds(block_rows + 2 * RIM + SUBLANES, SUBLANES), :] = line
    for side in (side_u, side_v, side_a, side_b, side_t):
        side[pl.ds(0, SUBLANES), :] = line
        side[pl.ds(rows + 2 * RIM + SUBLANES, SUBLANES), :] = line

    @pl.when(has_south)
    def _():
        for copy in lat_ups:
            copy.wait_recv()

    @pl.when(has_north)
    def _():
        for copy in lat_downs:
            copy.wait_recv()

    core = lax.rem(me, 2)
    chip = me // 2
    chips = lats // 2

    def hop_of(step, core):
        sign = jnp.where(core == 0, 1, chips - 1)
        hop = jnp.where((step == 0) | (step == 4), sign, 0)
        hop = jnp.where((step == 1) | (step == 3), 2, hop)
        return jnp.where((step == 2) | (step == 5), chips - sign, hop)

    def swap_of(step):
        return jnp.where((step >= 3) & (step <= 6), 1, 0)

    def taker_of(step):
        lat_chip = lax.rem(chip + hop_of(step, core), chips)
        return lat_chip * 2 + lax.rem(core + swap_of(step), 2)

    def giver_of(step):
        other = lax.rem(core + swap_of(step), 2)
        return lax.rem(chip + chips - hop_of(step, other), chips) * 2 + other

    def route_copy(step, lat, slot):
        return pltpu.make_async_remote_copy(
            src_ref=outbox.at[lat],
            dst_ref=blocks.at[slot],
            send_sem=route_send.at[step],
            recv_sem=route_recv.at[step],
            device_id=(lat, here),
            device_id_type=MESH,
        )

    def side_copy(step, lat, slot):
        return pltpu.make_async_remote_copy(
            src_ref=side_out.at[lat],
            dst_ref=side_in.at[slot],
            send_sem=side_send.at[step],
            recv_sem=side_recv.at[step],
            device_id=(lat, here),
            device_id_type=MESH,
        )

    right_end = lane == LANES - 1
    left_end = lane == 0

    def across(tiles):
        ahead = [spin(cells, -1) for cells in tiles]
        behind = [spin(cells, 1) for cells in tiles]
        return [
            jnp.where(right_end, ahead[1 - t], ahead[t])
            - jnp.where(left_end, behind[1 - t], behind[t])
            for t in range(2)
        ]

    def around_row(group):
        row = (group + 1) * SUBLANES
        return [pl.ds(row + shift, SUBLANES) for shift in (0, 1, -1)]

    def subcycles(target):
        base = order[target] * block_groups

        def fixed(field, tile, group):
            return ext[field, tile, base + group]

        for group in range(block_groups + 2 * EDGE):
            at = around_row(group)[0]
            for tile in range(2):
                work_u[tile, at, :] = fixed(U, tile, group)
                work_v[tile, at, :] = fixed(V, tile, group)

        for level in range(count):
            stress_span, momentum_span = reaches(count, level, block_rows)
            for group in stress_span:
                at, over, under = around_row(group)
                u_x = across([work_u[t, at, :] for t in range(2)])
                v_x = across([work_v[t, at, :] for t in range(2)])
                for t in range(2):
                    u_y = work_u[t, over, :] - work_u[t, under, :]
                    v_y = work_v[t, over, :] - work_v[t, under, :]
                    if level == 0:
                        old = [fixed(field, t, group) for field in (A, B, T)]
                    else:
                        old = [work[t, at, :] for work in (work_a, work_b, work_t)]
                    c, q = fixed(C + level, t, group), fixed(Q, t, group)
                    new = stress(u_x[t], u_y, v_x[t], v_y, *old, c, q)
                    for work, cells in zip((work_a, work_b, work_t), new):
                        work[t, at, :] = cells
            final = level == count - 1
            for group in momentum_span:
                at, over, under = around_row(group)
                here_a = [work_a[t, at, :] for t in range(2)]
                here_t = [work_t[t, at, :] for t in range(2)]
                a_x, t_x = across(here_a), across(here_t)
                for t in range(2):
                    f_x = a_x[t] + (work_t[t, over, :] - work_t[t, under, :])
                    f_y = t_x[t] + (work_b[t, over, :] - work_b[t, under, :])
                    new = momentum(
                        work_u[t, at, :],
                        work_v[t, at, :],
                        f_x,
                        f_y,
                        fixed(Q, t, group),
                        fixed(GX, t, group),
                        fixed(GY, t, group),
                    )
                    if final:
                        done = finish(*new, here_a[t], work_b[t, at, :], here_t[t])
                        inside = pl.ds((group - EDGE) * SUBLANES, SUBLANES)
                        for part, cells in enumerate(done):
                            outbox[target, part, inside, pl.ds(t * LANES, LANES)] = cells
                    else:
                        work_u[t, at, :], work_v[t, at, :] = new

    held = lats - 3

    def deliver(step, _):
        lat = taker_of(step)
        subcycles(lat)

        @pl.when((step < lats - 1) & (step != held))
        def _():
            route_copy(step, lat, me).start()

        return 0

    lax.fori_loop(0, lats - 2, deliver, 0)

    for copy in lon_both:
        copy.wait_recv()

    @pl.when(has_south)
    def _():
        for copy in lon_ups:
            copy.wait_recv()

    @pl.when(has_north)
    def _():
        for copy in lon_downs:
            copy.wait_recv()

    def unpack(group, names, beyond):
        from_east, from_west = rim_east[group], rim_west[group]
        for field in names:
            start, other = places[field]
            width = widths[field]
            if other == (HALF + start - width) % LANES:
                end = (start + HALF // 2) % LANES
                if start < end:
                    mine = (lane >= start) & (lane < end)
                else:
                    mine = (lane >= start) | (lane < end)
                rim = spin(jnp.where(mine, from_east, from_west), HALF - start)
            else:
                rim = jnp.where(
                    lane < LANES - HALF // 2,
                    spin(from_east, HALF - start),
                    spin(from_west, -other - width),
                )
            if beyond:
                base = fold(ext[field, 0, group], ext[field, 1, group])
            else:
                base = get_side(field, group)
            put_side(field, group, jnp.where(lane < HALF, base, rim))

    for group in (0, groups + 2 * EDGE - 1):
        unpack(group, range(far), True)
    for group in (1, groups + 2 * EDGE - 2):
        unpack(group, range(fields), True)

    def unpack_inside(group, _):
        unpack(group, range(fields), False)
        return 0

    lax.fori_loop(EDGE, groups + EDGE, unpack_inside, 0, unroll=8)

    def beside(cells):
        return spin(cells, -1) - spin(cells, 1)

    def middle_of(part):
        return 2 * deep * part + deep

    for level in range(count):
        stress_span, momentum_span = reaches(count, level, rows)
        for group in stress_span:
            at, over, under = around_row(group)
            new = stress(
                beside(side_u[at, :]),
                side_u[over, :] - side_u[under, :],
                beside(side_v[at, :]),
                side_v[over, :] - side_v[under, :],
                side_a[at, :],
                side_b[at, :],
                side_t[at, :],
                side_fixed[C + level - MOVING, group],
                side_fixed[Q - MOVING, group],
            )
            side_a[at, :], side_b[at, :], side_t[at, :] = new
        for group in momentum_span:
            at, over, under = around_row(group)
            a, b, t = side_a[at, :], side_b[at, :], side_t[at, :]
            new = momentum(
                side_u[at, :],
                side_v[at, :],
                beside(a) + (side_t[over, :] - side_t[under, :]),
                beside(t) + (side_b[over, :] - side_b[under, :]),
                side_fixed[Q - MOVING, group],
                side_fixed[GX - MOVING, group],
                side_fixed[GY - MOVING, group],
            )
            if level < count - 1:
                side_u[at, :], side_v[at, :] = new
            else:
                parts = []
                for part, cells in enumerate(finish(*new, a, b, t)):
                    cells = jnp.where(lane < HALF // 2, cells, spin(cells, HALF))
                    start = middle_of(part) - deep
                    parts.append((start, 2 * deep, spin(cells, middle_of(part))))
                sides[group - EDGE] = lay(lane, parts)

    def deliver_sides(step, _):
        lat = taker_of(step)
        base = order[lat] * block_groups
        for group in range(block_groups):
            side_out[lat, group] = sides[base + group]

        @pl.when(step < lats - 1)
        def _():
            side_copy(step, lat, me).start()

        return 0

    lax.fori_loop(0, lats, deliver_sides, 0)
    route_copy(held, taker_of(held), me).start()
    lax.fori_loop(lats - 2, lats, deliver, 0)

    own = pltpu.make_async_copy(outbox.at[me], blocks.at[me], own_sem)
    own.start()

    def place(packed, part, tiles):
        moved = spin(packed, -middle_of(part))
        return (
            jnp.where(lane < deep, moved, tiles[0]),
            jnp.where(lane >= LANES - deep, moved, tiles[1]),
        )

    both_lanes = [pl.ds(tile * LANES, LANES) for tile in range(2)]

    def exchange(j, _):
        taker = route[me, j]
        for part in range(block_groups):
            at = pl.ds(part * SUBLANES, SUBLANES)
            group = j * block_groups + part
            row = pl.multiple_of(group * SUBLANES, SUBLANES)
            for axis in range(2):
                drift = [outbox[taker, axis, at, lanes] for lanes in both_lanes]
                drift = place(sides[group], axis, drift)
                for tile, lanes in enumerate(both_lanes):
                    icy = ext[Q, tile, group + EDGE] > 0.0
                    moved = drift[tile] - raw_force[2 + axis, group, :, lanes]
                    flux[axis, pl.ds(row, SUBLANES), lanes] = jnp.where(icy, DRAG_COEF * moved, 0.0)
        return 0

    lax.fori_loop(0, lats, exchange, 0)

    def mend(slot, source):
        for group in range(block_groups):
            packed = source[slot, group]
            at = pl.ds(group * SUBLANES, SUBLANES)
            for part in range(MOVING):
                tiles = place(packed, part, [blocks[slot, part, at, lanes] for lanes in both_lanes])
                for lanes, cells in zip(both_lanes, tiles):
                    blocks[slot, part, at, lanes] = cells

    own.wait()
    mend(me, side_out)

    def receive(turn, _):
        step = jnp.where(turn < held, turn, jnp.where(turn == held, held + 1, held))
        lat = giver_of(step)
        route_copy(step, lat, lat).wait_recv()
        side_copy(step, lat, lat).wait_recv()
        mend(lat, side_in)
        return 0

    lax.fori_loop(0, lats - 1, receive, 0)

    def settle(step, _):
        route_copy(step, taker_of(step), me).wait_send()
        side_copy(step, taker_of(step), me).wait_send()
        return 0

    lax.fori_loop(0, lats - 1, settle, 0)

    for copy in lon_both:
        copy.wait_send()

    @pl.when(has_north)
    def _():
        for copy in lat_ups + lon_ups:
            copy.wait_send()

    @pl.when(has_south)
    def _():
        for copy in lat_downs + lon_downs:
            copy.wait_send()


def hand_out(flux, blocks, flux_out, blocks_out, sems):
    copies = [
        pltpu.make_async_copy(flux, flux_out, sems.at[0]),
        pltpu.make_async_copy(blocks, blocks_out, sems.at[1]),
    ]
    for copy in copies:
        copy.start()
    for copy in copies:
        copy.wait()


def per_device(lats, lons, ice_state, ocean_forcing, ice_strength, ice_mask, yield_mask, ice_route):
    count, rows, columns = yield_mask.shape
    block_rows = rows // lats
    fields = C + count
    groups = rows // SUBLANES
    f32, i32 = jnp.float32, jnp.int32
    as_is = pl.BlockSpec(memory_space=pl.ANY)
    vmem = pl.BlockSpec(memory_space=pltpu.VMEM)
    dma = pltpu.SemaphoreType.DMA

    def tiles(*lead, kind=f32, wide=LANES):
        return pltpu.VMEM(lead + (SUBLANES, wide), kind)

    def split(cells):
        return cells.reshape(cells.shape[:-2] + (groups, SUBLANES, columns))

    work = pltpu.VMEM((2, block_rows + 2 * RIM + 2 * SUBLANES, LANES), f32)
    side = pltpu.VMEM((rows + 2 * RIM + 2 * SUBLANES, LANES), f32)
    shapes = ((2, rows, columns), (lats, 5, block_rows, columns))
    results = pl.pallas_call(
        functools.partial(kernel, count, lats, lons),
        out_shape=tuple(pltpu.VMEM(shape, f32) for shape in shapes),
        in_specs=[as_is] * 6,
        out_specs=(vmem, vmem),
        scratch_shapes=[
            tiles(5, groups, wide=columns),
            tiles(4, groups, wide=columns),
            tiles(groups, wide=columns),
            tiles(groups, kind=i32, wide=columns),
            tiles(count, groups, kind=i32, wide=columns),
            tiles(fields, 2, groups + 2 * EDGE),
            tiles(groups),
            tiles(groups),
            tiles(groups + 2 * EDGE),
            tiles(groups + 2 * EDGE),
            work,
            work,
            work,
            work,
            work,
            side,
            side,
            side,
            side,
            side,
            tiles(fields - MOVING, groups + 2 * EDGE),
            tiles(groups),
            pltpu.VMEM((lats, 5, block_rows, columns), f32),
            tiles(lats, block_rows // SUBLANES),
            tiles(lats, block_rows // SUBLANES),
            pltpu.SMEM((lats, lats), i32),
            pltpu.SMEM((lats,), i32),
            dma((21,)),
            dma((10,)),
            dma((10,)),
            dma((lats - 1,)),
            dma((lats - 1,)),
            dma((lats - 1,)),
            dma((lats - 1,)),
            dma,
            pltpu.SemaphoreType.REGULAR,
        ],
        compiler_params=pltpu.CompilerParams(collective_id=0, has_side_effects=True),
        name="ice_step",
    )(
        ice_route,
        split(ice_state),
        split(ocean_forcing),
        split(ice_strength),
        split(ice_mask),
        split(yield_mask),
    )
    return pl.pallas_call(
        hand_out,
        out_shape=tuple(jax.ShapeDtypeStruct(shape, f32) for shape in shapes),
        in_specs=[as_is] * 2,
        out_specs=(as_is, as_is),
        scratch_shapes=[dma((2,))],
        compiler_params=pltpu.CompilerParams(vmem_limit_bytes=1 << 20),
        name="hand_out",
    )(*results)


def solution(mesh):
    return jax.shard_map(
        functools.partial(per_device, mesh.shape["lat"], mesh.shape["lon"]),
        mesh=mesh,
        in_specs=(
            P(None, "lat", "lon"),
            P(None, "lat", "lon"),
            P("lat", "lon"),
            P("lat", "lon"),
            P(None, "lat", "lon"),
            P(),
        ),
        out_specs=(P(None, "lat", "lon"), P("lat", None, None, "lon")),
        check_vma=False,
    )
```

```python
import functools

import jax
import jax.numpy as jnp
from jax import lax
from jax.experimental import pallas as pl
from jax.experimental.pallas import tpu as pltpu
from jax.sharding import PartitionSpec as P

RELAX_RATE = 1.0
STEP_WEIGHT = 0.5
DRAG_COEF = 0.5
CORIOLIS = 0.3

KEEP = 1.0 / (1.0 + RELAX_RATE)
DAMP = 1.0 / (1.0 + STEP_WEIGHT * DRAG_COEF)

MESH = pl.DeviceIdType.MESH
LANES = 128
HALF = LANES // 2
SUBLANES = 8
RIM = 16
EDGE = RIM // SUBLANES

U, V, A, B, T, Q, GX, GY, C = range(9)
MOVING = 5


def layout(count):
    deep = 2 * count
    widths = {U: deep, V: deep, A: deep - 1, T: deep - 1, Q: deep - 1, C: deep - 1}
    widths.update({B: deep - 2, GX: deep - 2, GY: deep - 2})
    for level in range(1, count):
        widths[C + level] = deep - 1 - 2 * level
    names = list(widths)

    def window(start, width):
        return {(start + i) % LANES for i in range(width)}

    def settle(index, to_west, to_east):
        if index == len(names):
            return {}
        width = widths[names[index]]
        for turn in range(LANES - width + 1):
            mine, other = window(turn, width), window(HALF + turn - width, width)
            if mine & to_west or other & to_east:
                continue
            rest = settle(index + 1, to_west | mine, to_east | other)
            if rest is not None:
                return {names[index]: (turn, (HALF + turn - width) % LANES), **rest}
            if index < len(names) - 3:
                return None
        free_west = [p for p in range(LANES - width + 1) if not window(p, width) & to_west]
        free_east = [p for p in range(LANES - width + 1) if not window(p, width) & to_east]
        if not free_west or not free_east:
            return None
        west, east = free_west[0], free_east[0]
        rest = settle(index + 1, to_west | window(west, width), to_east | window(east, width))
        return None if rest is None else {names[index]: (west, east), **rest}

    return widths, settle(0, set(), set())


def spin(cells, shift):
    shift = shift % LANES
    return cells if shift == 0 else pltpu.roll(cells, shift, 1)


def lay(lane, parts):
    parts = sorted(parts, key=lambda part: part[0])
    start, width, cells = parts[-1]
    total = cells if start + width > LANES else parts[0][2]
    for start, width, cells in parts:
        total = jnp.where(lane >= start, cells, total)
    return total


def stress(u_x, u_y, v_x, v_y, a, b, t, c, q):
    both = u_x + v_y
    next_a = KEEP * a + (c * (both + 2.0 * u_x) - q)
    next_b = KEEP * b + (c * (both + 2.0 * v_y) - q)
    return next_a, next_b, KEEP * t + c * (u_y + v_x)


def momentum(u, v, f_x, f_y, q, g_x, g_y):
    gain = jnp.where(q > 0.0, DAMP, 0.0)
    turn, push = STEP_WEIGHT * CORIOLIS, STEP_WEIGHT * 0.25
    next_u = gain * (u + (turn * v + push * f_x)) + g_x
    next_v = gain * (v + (push * f_y - turn * u)) + g_y
    return next_u, next_v


def finish(u, v, a, b, t):
    return u, v, 0.5 * (a + b), 0.5 * (a - b), 0.5 * t


def reaches(count, level, rows):
    reach = 2 * (count - 1 - level)

    def span(extra):
        low = (RIM - reach - extra) // SUBLANES
        high = -(-(RIM + rows + reach + extra) // SUBLANES)
        return range(low, high)

    return span(1), span(0)


def kernel(
    count,
    lats,
    lons,
    route_in,
    state,
    forcing,
    strength,
    mask,
    regime,
    flux,
    blocks,
    raw_state,
    raw_force,
    raw_strength,
    raw_mask,
    raw_regime,
    ext,
    pack_west,
    pack_east,
    rim_east,
    rim_west,
    work_u,
    work_v,
    work_a,
    work_b,
    work_t,
    side_u,
    side_v,
    side_a,
    side_b,
    side_t,
    side_fixed,
    sides,
    outbox,
    side_out,
    side_in,
    route,
    order,
    load_sem,
    rim_send,
    rim_recv,
    route_send,
    route_recv,
    side_send,
    side_recv,
    own_sem,
    ready,
):
    fields = C + count
    widths, places = layout(count)
    groups = state.shape[1]
    rows = groups * SUBLANES
    block_rows = rows // lats
    block_groups = block_rows // SUBLANES
    deep = 2 * count
    me = lax.axis_index("lat")
    here = lax.axis_index("lon")
    west = lax.rem(here + lons - 1, lons)
    east = lax.rem(here + 1, lons)
    north = lax.rem(me + lats - 1, lats)
    south = lax.rem(me + 1, lats)
    odd = lax.rem(here, 2)

    barrier = pltpu.get_barrier_semaphore()
    for step in range(1, lats):
        pl.semaphore_signal(
            barrier, inc=1, device_id=(lax.rem(me + step, lats), here), device_id_type=MESH
        )
    around = [(lat, lon) for lon in (west, east) for lat in (north, me, south)]

    loads = []

    def load(src, dst):
        copy = pltpu.make_async_copy(src, dst, load_sem.at[len(loads)])
        copy.start()
        loads.append(copy)

    def load_groups(at):
        first = len(loads)
        load(state.at[:, at], raw_state.at[:, at])
        load(forcing.at[:, at], raw_force.at[:, at])
        load(strength.at[at], raw_strength.at[at])
        load(mask.at[at], raw_mask.at[at])
        load(regime.at[:, at], raw_regime.at[:, at])
        return loads[first:]

    half = (groups - 2 * EDGE) // 2
    chunks = [
        load_groups(pl.ds(0, EDGE)),
        load_groups(pl.ds(groups - EDGE, EDGE)),
        load_groups(pl.ds(EDGE, half)),
        load_groups(pl.ds(EDGE + half, groups - 2 * EDGE - half)),
    ]
    load(route_in, route)

    lane = lax.broadcasted_iota(jnp.int32, (SUBLANES, LANES), 1)
    right_part = (lane >= HALF // 2) & (lane < HALF)

    def fold(left, right):
        return jnp.where(right_part, spin(right, HALF), left)

    side_moving = (side_u, side_v, side_a, side_b, side_t)

    def side_rows(group):
        row = (group + 1) * SUBLANES
        return pl.ds(row if isinstance(group, int) else pl.multiple_of(row, SUBLANES), SUBLANES)

    def put_side(field, group, cells):
        if field < MOVING:
            side_moving[field][side_rows(group), :] = cells
        else:
            side_fixed[field - MOVING, group] = cells

    def get_side(field, group):
        if field < MOVING:
            return side_moving[field][side_rows(group), :]
        return side_fixed[field - MOVING, group]

    def prepare(at, _):
        made = []
        for tile in range(2):
            lanes = pl.ds(tile * LANES, LANES)
            ice = raw_mask[at, :, lanes].astype(jnp.float32)
            firm = ice * raw_strength[at, :, lanes]
            s1 = ice * raw_state[2, at, :, lanes]
            s2 = ice * raw_state[3, at, :, lanes]
            push = (STEP_WEIGHT * DAMP) * ice
            low = firm * (KEEP * 0.125)
            cells = {
                U: raw_state[0, at, :, lanes],
                V: raw_state[1, at, :, lanes],
                A: s1 + s2,
                B: s1 - s2,
                T: (2.0 * ice) * raw_state[4, at, :, lanes],
                Q: firm * (KEEP * 0.5),
                GX: push * (raw_force[0, at, :, lanes] + DRAG_COEF * raw_force[2, at, :, lanes]),
                GY: push * (raw_force[1, at, :, lanes] + DRAG_COEF * raw_force[3, at, :, lanes]),
            }
            for level in range(count):
                stiff = 3.0 - 2.0 * raw_regime[level, at, :, lanes].astype(jnp.float32)
                cells[C + level] = low * stiff
            for field in range(fields):
                ext[field, tile, at + EDGE] = cells[field]
            made.append(cells)
        to_west, to_east = [], []
        for field, (start, other) in places.items():
            width = widths[field]
            both = fold(made[0][field], made[1][field])
            put_side(field, at + EDGE, both)
            moved = spin(both, start)
            to_west.append((start, width, moved))
            if other != (HALF + start - width) % LANES:
                moved = spin(both, other + width - HALF)
            to_east.append((other, width, moved))
        pack_west[at] = lay(lane, to_west)
        pack_east[at] = lay(lane, to_east)
        return 0

    def copies_done(chunk):
        for copy in chunk:
            copy.wait()

    copies_done(chunks[0] + chunks[1])
    for end in (0, groups - EDGE):
        for group in range(EDGE):
            prepare(end + group, 0)

    def rim_copy(index, src, dst, lat, lon):
        return pltpu.make_async_remote_copy(
            src_ref=src,
            dst_ref=dst,
            send_sem=rim_send.at[index],
            recv_sem=rim_recv.at[index],
            device_id=(lat, lon),
            device_id_type=MESH,
        )

    far = C + sum(1 for level in range(count) if deep - 1 - 2 * level > SUBLANES)
    near_count = fields - far
    top, bottom = pl.ds(0, EDGE), pl.ds(EDGE + groups, EDGE)
    first, last = pl.ds(0, EDGE), pl.ds(groups - EDGE, EDGE)
    wide_fields, late_fields = pl.ds(0, far), pl.ds(far, near_count)

    def lat_copy(index, part, src, dst, lat):
        return rim_copy(index, ext.at[part, :, src], ext.at[part, :, dst], lat, here)

    lat_ups = [
        lat_copy(0, wide_fields, pl.ds(EDGE, EDGE), bottom, north),
        lat_copy(1, late_fields, pl.ds(EDGE, 1), pl.ds(EDGE + groups, 1), north),
    ]
    lat_downs = [
        lat_copy(2, wide_fields, pl.ds(groups, EDGE), top, south),
        lat_copy(3, late_fields, pl.ds(groups + EDGE - 1, 1), pl.ds(EDGE - 1, 1), south),
    ]

    def lon_copies(index, start, size):
        src, dst = pl.ds(start, size), pl.ds(start + EDGE, size)
        return [
            rim_copy(index, pack_west.at[src], rim_east.at[dst], me, west),
            rim_copy(index + 1, pack_east.at[src], rim_west.at[dst], me, east),
        ]

    lon_early = lon_copies(4, 0, EDGE + half)
    lon_late = lon_copies(10, EDGE + half, groups - EDGE - half)
    lon_both = lon_early + lon_late
    lon_ups = [
        rim_copy(6, pack_west.at[first], rim_east.at[bottom], north, west),
        rim_copy(7, pack_east.at[first], rim_west.at[bottom], north, east),
    ]
    lon_downs = [
        rim_copy(8, pack_west.at[last], rim_east.at[top], south, west),
        rim_copy(9, pack_east.at[last], rim_west.at[top], south, east),
    ]
    has_north, has_south = me > 0, me < lats - 1

    @pl.when(odd == 0)
    def _():
        pl.semaphore_wait(barrier, lats - 1)

    @pl.when(odd == 1)
    def _():
        pl.semaphore_wait(barrier, lats - 1 + len(around))

    @pl.when(has_north)
    def _():
        for copy in lat_ups:
            copy.start()

    @pl.when(has_south)
    def _():
        for copy in lat_downs:
            copy.start()

    @pl.when(odd == 0)
    def _():
        for target in around:
            pl.semaphore_signal(barrier, inc=1, device_id=target, device_id_type=MESH)

    @pl.when(odd == 1)
    def _():
        for target in around:
            pl.semaphore_signal(ready, inc=1, device_id=target, device_id_type=MESH)

    def send_lon(part):
        for copy in part:
            copy.start()

    copies_done(chunks[2])
    lax.fori_loop(EDGE, EDGE + half, prepare, 0, unroll=7)

    @pl.when(odd == 1)
    def _():
        send_lon(lon_early)

    copies_done(chunks[3])
    lax.fori_loop(EDGE + half, groups - EDGE, prepare, 0, unroll=7)

    def send_corners():
        @pl.when(has_north)
        def _():
            for copy in lon_ups:
                copy.start()

        @pl.when(has_south)
        def _():
            for copy in lon_downs:
                copy.start()

    @pl.when(odd == 1)
    def _():
        send_lon(lon_late)
        send_corners()

    loads[-1].wait()
    for lat in range(lats):
        block = jnp.int32(0)
        for j in range(1, lats):
            apart = route[me, j] - lat
            block = block + j * (1 - lax.div(apart * apart + 63, 64))
        order[lat] = lax.rem(block, lats)

    def blank(at):
        nothing = jnp.zeros((EDGE, SUBLANES, LANES), jnp.float32)
        rim_east[at] = nothing
        rim_west[at] = nothing
        for field in range(fields):
            for tile in range(2):
                ext[field, tile, at] = nothing

    @pl.when(me == 0)
    def _():
        blank(top)

    @pl.when(me == lats - 1)
    def _():
        blank(bottom)

    line = jnp.zeros((SUBLANES, LANES), jnp.float32)
    for work in (work_u, work_v, work_a, work_b, work_t):
        for tile in range(2):
            work[tile, pl.ds(0, SUBLANES), :] = line
            work[tile, pl.ds(block_rows + 2 * RIM + SUBLANES, SUBLANES), :] = line
    for side in (side_u, side_v, side_a, side_b, side_t):
        side[pl.ds(0, SUBLANES), :] = line
        side[pl.ds(rows + 2 * RIM + SUBLANES, SUBLANES), :] = line

    @pl.when(has_south)
    def _():
        for copy in lat_ups:
            copy.wait_recv()

    @pl.when(has_north)
    def _():
        for copy in lat_downs:
            copy.wait_recv()

    core = lax.rem(me, 2)
    chip = me // 2
    chips = lats // 2

    def hop_of(step, core):
        sign = jnp.where(core == 0, 1, chips - 1)
        hop = jnp.where((step == 0) | (step == 4), sign, 0)
        hop = jnp.where((step == 1) | (step == 3), 2, hop)
        return jnp.where((step == 2) | (step == 5), chips - sign, hop)

    def swap_of(step):
        return jnp.where((step >= 3) & (step <= 6), 1, 0)

    def taker_of(step):
        lat_chip = lax.rem(chip + hop_of(step, core), chips)
        return lat_chip * 2 + lax.rem(core + swap_of(step), 2)

    def giver_of(step):
        other = lax.rem(core + swap_of(step), 2)
        return lax.rem(chip + chips - hop_of(step, other), chips) * 2 + other

    def route_copy(step, lat, slot):
        return pltpu.make_async_remote_copy(
            src_ref=outbox.at[lat],
            dst_ref=blocks.at[slot],
            send_sem=route_send.at[step],
            recv_sem=route_recv.at[step],
            device_id=(lat, here),
            device_id_type=MESH,
        )

    def side_copy(step, lat, slot):
        return pltpu.make_async_remote_copy(
            src_ref=side_out.at[lat],
            dst_ref=side_in.at[slot],
            send_sem=side_send.at[step],
            recv_sem=side_recv.at[step],
            device_id=(lat, here),
            device_id_type=MESH,
        )

    right_end = lane == LANES - 1
    left_end = lane == 0

    def across(tiles):
        ahead = [spin(cells, -1) for cells in tiles]
        behind = [spin(cells, 1) for cells in tiles]
        return [
            jnp.where(right_end, ahead[1 - t], ahead[t])
            - jnp.where(left_end, behind[1 - t], behind[t])
            for t in range(2)
        ]

    def around_row(group):
        row = (group + 1) * SUBLANES
        return [pl.ds(row + shift, SUBLANES) for shift in (0, 1, -1)]

    def subcycles(target):
        base = order[target] * block_groups

        def fixed(field, tile, group):
            return ext[field, tile, base + group]

        for group in range(block_groups + 2 * EDGE):
            at = around_row(group)[0]
            for tile in range(2):
                work_u[tile, at, :] = fixed(U, tile, group)
                work_v[tile, at, :] = fixed(V, tile, group)

        for level in range(count):
            stress_span, momentum_span = reaches(count, level, block_rows)
            for group in stress_span:
                at, over, under = around_row(group)
                u_x = across([work_u[t, at, :] for t in range(2)])
                v_x = across([work_v[t, at, :] for t in range(2)])
                for t in range(2):
                    u_y = work_u[t, over, :] - work_u[t, under, :]
                    v_y = work_v[t, over, :] - work_v[t, under, :]
                    if level == 0:
                        old = [fixed(field, t, group) for field in (A, B, T)]
                    else:
                        old = [work[t, at, :] for work in (work_a, work_b, work_t)]
                    c, q = fixed(C + level, t, group), fixed(Q, t, group)
                    new = stress(u_x[t], u_y, v_x[t], v_y, *old, c, q)
                    for work, cells in zip((work_a, work_b, work_t), new):
                        work[t, at, :] = cells
            final = level == count - 1
            for group in momentum_span:
                at, over, under = around_row(group)
                here_a = [work_a[t, at, :] for t in range(2)]
                here_t = [work_t[t, at, :] for t in range(2)]
                a_x, t_x = across(here_a), across(here_t)
                for t in range(2):
                    f_x = a_x[t] + (work_t[t, over, :] - work_t[t, under, :])
                    f_y = t_x[t] + (work_b[t, over, :] - work_b[t, under, :])
                    new = momentum(
                        work_u[t, at, :],
                        work_v[t, at, :],
                        f_x,
                        f_y,
                        fixed(Q, t, group),
                        fixed(GX, t, group),
                        fixed(GY, t, group),
                    )
                    if final:
                        done = finish(*new, here_a[t], work_b[t, at, :], here_t[t])
                        inside = pl.ds((group - EDGE) * SUBLANES, SUBLANES)
                        for part, cells in enumerate(done):
                            outbox[target, part, inside, pl.ds(t * LANES, LANES)] = cells
                    else:
                        work_u[t, at, :], work_v[t, at, :] = new

    held = lats - 3

    answered = 2

    def deliver(step, _):
        lat = taker_of(step)

        @pl.when((odd == 0) & (step == answered))
        def _():
            pl.semaphore_wait(ready, len(around))
            send_lon(lon_both)
            send_corners()

        subcycles(lat)

        @pl.when((step < lats - 1) & (step != held))
        def _():
            route_copy(step, lat, me).start()

        return 0

    lax.fori_loop(0, lats - 2, deliver, 0)

    for copy in lon_both:
        copy.wait_recv()

    @pl.when(has_south)
    def _():
        for copy in lon_ups:
            copy.wait_recv()

    @pl.when(has_north)
    def _():
        for copy in lon_downs:
            copy.wait_recv()

    def unpack(group, names, beyond):
        from_east, from_west = rim_east[group], rim_west[group]
        for field in names:
            start, other = places[field]
            width = widths[field]
            if other == (HALF + start - width) % LANES:
                end = (start + HALF // 2) % LANES
                if start < end:
                    mine = (lane >= start) & (lane < end)
                else:
                    mine = (lane >= start) | (lane < end)
                rim = spin(jnp.where(mine, from_east, from_west), HALF - start)
            else:
                rim = jnp.where(
                    lane < LANES - HALF // 2,
                    spin(from_east, HALF - start),
                    spin(from_west, -other - width),
                )
            if beyond:
                base = fold(ext[field, 0, group], ext[field, 1, group])
            else:
                base = get_side(field, group)
            put_side(field, group, jnp.where(lane < HALF, base, rim))

    for group in (0, groups + 2 * EDGE - 1):
        unpack(group, range(far), True)
    for group in (1, groups + 2 * EDGE - 2):
        unpack(group, range(fields), True)

    def unpack_inside(group, _):
        unpack(group, range(fields), False)
        return 0

    lax.fori_loop(EDGE, groups + EDGE, unpack_inside, 0, unroll=8)

    def beside(cells):
        return spin(cells, -1) - spin(cells, 1)

    def middle_of(part):
        return 2 * deep * part + deep

    for level in range(count):
        stress_span, momentum_span = reaches(count, level, rows)
        for group in stress_span:
            at, over, under = around_row(group)
            new = stress(
                beside(side_u[at, :]),
                side_u[over, :] - side_u[under, :],
                beside(side_v[at, :]),
                side_v[over, :] - side_v[under, :],
                side_a[at, :],
                side_b[at, :],
                side_t[at, :],
                side_fixed[C + level - MOVING, group],
                side_fixed[Q - MOVING, group],
            )
            side_a[at, :], side_b[at, :], side_t[at, :] = new
        for group in momentum_span:
            at, over, under = around_row(group)
            a, b, t = side_a[at, :], side_b[at, :], side_t[at, :]
            new = momentum(
                side_u[at, :],
                side_v[at, :],
                beside(a) + (side_t[over, :] - side_t[under, :]),
                beside(t) + (side_b[over, :] - side_b[under, :]),
                side_fixed[Q - MOVING, group],
                side_fixed[GX - MOVING, group],
                side_fixed[GY - MOVING, group],
            )
            if level < count - 1:
                side_u[at, :], side_v[at, :] = new
            else:
                parts = []
                for part, cells in enumerate(finish(*new, a, b, t)):
                    cells = jnp.where(lane < HALF // 2, cells, spin(cells, HALF))
                    start = middle_of(part) - deep
                    parts.append((start, 2 * deep, spin(cells, middle_of(part))))
                sides[group - EDGE] = lay(lane, parts)

    def deliver_sides(step, _):
        lat = taker_of(step)
        base = order[lat] * block_groups
        for group in range(block_groups):
            side_out[lat, group] = sides[base + group]

        @pl.when(step < lats - 1)
        def _():
            side_copy(step, lat, me).start()

        return 0

    lax.fori_loop(0, lats, deliver_sides, 0)
    route_copy(held, taker_of(held), me).start()
    lax.fori_loop(lats - 2, lats, deliver, 0)

    own = pltpu.make_async_copy(outbox.at[me], blocks.at[me], own_sem)
    own.start()

    def place(packed, part, tiles):
        moved = spin(packed, -middle_of(part))
        return (
            jnp.where(lane < deep, moved, tiles[0]),
            jnp.where(lane >= LANES - deep, moved, tiles[1]),
        )

    both_lanes = [pl.ds(tile * LANES, LANES) for tile in range(2)]

    def exchange(j, _):
        taker = route[me, j]
        for part in range(block_groups):
            at = pl.ds(part * SUBLANES, SUBLANES)
            group = j * block_groups + part
            row = pl.multiple_of(group * SUBLANES, SUBLANES)
            for axis in range(2):
                drift = [outbox[taker, axis, at, lanes] for lanes in both_lanes]
                drift = place(sides[group], axis, drift)
                for tile, lanes in enumerate(both_lanes):
                    icy = ext[Q, tile, group + EDGE] > 0.0
                    moved = drift[tile] - raw_force[2 + axis, group, :, lanes]
                    flux[axis, pl.ds(row, SUBLANES), lanes] = jnp.where(icy, DRAG_COEF * moved, 0.0)
        return 0

    lax.fori_loop(0, lats, exchange, 0)

    def mend(slot, source):
        for group in range(block_groups):
            packed = source[slot, group]
            at = pl.ds(group * SUBLANES, SUBLANES)
            for part in range(MOVING):
                tiles = place(packed, part, [blocks[slot, part, at, lanes] for lanes in both_lanes])
                for lanes, cells in zip(both_lanes, tiles):
                    blocks[slot, part, at, lanes] = cells

    own.wait()
    mend(me, side_out)

    def receive(turn, _):
        step = jnp.where(turn < held, turn, jnp.where(turn == held, held + 1, held))
        lat = giver_of(step)
        route_copy(step, lat, lat).wait_recv()
        side_copy(step, lat, lat).wait_recv()
        mend(lat, side_in)
        return 0

    lax.fori_loop(0, lats - 1, receive, 0)

    def settle(step, _):
        route_copy(step, taker_of(step), me).wait_send()
        side_copy(step, taker_of(step), me).wait_send()
        return 0

    lax.fori_loop(0, lats - 1, settle, 0)

    for copy in lon_both:
        copy.wait_send()

    @pl.when(has_north)
    def _():
        for copy in lat_ups + lon_ups:
            copy.wait_send()

    @pl.when(has_south)
    def _():
        for copy in lat_downs + lon_downs:
            copy.wait_send()


def hand_out(flux, blocks, flux_out, blocks_out, sems):
    copies = [
        pltpu.make_async_copy(flux, flux_out, sems.at[0]),
        pltpu.make_async_copy(blocks, blocks_out, sems.at[1]),
    ]
    for copy in copies:
        copy.start()
    for copy in copies:
        copy.wait()


def per_device(lats, lons, ice_state, ocean_forcing, ice_strength, ice_mask, yield_mask, ice_route):
    count, rows, columns = yield_mask.shape
    block_rows = rows // lats
    fields = C + count
    groups = rows // SUBLANES
    f32, i32 = jnp.float32, jnp.int32
    as_is = pl.BlockSpec(memory_space=pl.ANY)
    vmem = pl.BlockSpec(memory_space=pltpu.VMEM)
    dma = pltpu.SemaphoreType.DMA

    def tiles(*lead, kind=f32, wide=LANES):
        return pltpu.VMEM(lead + (SUBLANES, wide), kind)

    def split(cells):
        return cells.reshape(cells.shape[:-2] + (groups, SUBLANES, columns))

    work = pltpu.VMEM((2, block_rows + 2 * RIM + 2 * SUBLANES, LANES), f32)
    side = pltpu.VMEM((rows + 2 * RIM + 2 * SUBLANES, LANES), f32)
    shapes = ((2, rows, columns), (lats, 5, block_rows, columns))
    results = pl.pallas_call(
        functools.partial(kernel, count, lats, lons),
        out_shape=tuple(pltpu.VMEM(shape, f32) for shape in shapes),
        in_specs=[as_is] * 6,
        out_specs=(vmem, vmem),
        scratch_shapes=[
            tiles(5, groups, wide=columns),
            tiles(4, groups, wide=columns),
            tiles(groups, wide=columns),
            tiles(groups, kind=i32, wide=columns),
            tiles(count, groups, kind=i32, wide=columns),
            tiles(fields, 2, groups + 2 * EDGE),
            tiles(groups),
            tiles(groups),
            tiles(groups + 2 * EDGE),
            tiles(groups + 2 * EDGE),
            work,
            work,
            work,
            work,
            work,
            side,
            side,
            side,
            side,
            side,
            tiles(fields - MOVING, groups + 2 * EDGE),
            tiles(groups),
            pltpu.VMEM((lats, 5, block_rows, columns), f32),
            tiles(lats, block_rows // SUBLANES),
            tiles(lats, block_rows // SUBLANES),
            pltpu.SMEM((lats, lats), i32),
            pltpu.SMEM((lats,), i32),
            dma((21,)),
            dma((12,)),
            dma((12,)),
            dma((lats - 1,)),
            dma((lats - 1,)),
            dma((lats - 1,)),
            dma((lats - 1,)),
            dma,
            pltpu.SemaphoreType.REGULAR,
        ],
        compiler_params=pltpu.CompilerParams(collective_id=0, has_side_effects=True),
        name="ice_step",
    )(
        ice_route,
        split(ice_state),
        split(ocean_forcing),
        split(ice_strength),
        split(ice_mask),
        split(yield_mask),
    )
    return pl.pallas_call(
        hand_out,
        out_shape=tuple(jax.ShapeDtypeStruct(shape, f32) for shape in shapes),
        in_specs=[as_is] * 2,
        out_specs=(as_is, as_is),
        scratch_shapes=[dma((2,))],
        compiler_params=pltpu.CompilerParams(vmem_limit_bytes=1 << 20),
        name="hand_out",
    )(*results)


def solution(mesh):
    return jax.shard_map(
        functools.partial(per_device, mesh.shape["lat"], mesh.shape["lon"]),
        mesh=mesh,
        in_specs=(
            P(None, "lat", "lon"),
            P(None, "lat", "lon"),
            P("lat", "lon"),
            P("lat", "lon"),
            P(None, "lat", "lon"),
            P(),
        ),
        out_specs=(P(None, "lat", "lon"), P("lat", None, None, "lon")),
        check_vma=False,
    )
```

```python
import functools

import jax
import jax.numpy as jnp
from jax import lax
from jax.experimental import pallas as pl
from jax.experimental.pallas import tpu as pltpu
from jax.sharding import PartitionSpec as P

RELAX_RATE = 1.0
STEP_WEIGHT = 0.5
DRAG_COEF = 0.5
CORIOLIS = 0.3

KEEP = 1.0 / (1.0 + RELAX_RATE)
DAMP = 1.0 / (1.0 + STEP_WEIGHT * DRAG_COEF)

MESH = pl.DeviceIdType.MESH
LANES = 128
HALF = LANES // 2
SUBLANES = 8
RIM = 16
EDGE = RIM // SUBLANES
HELD = 1

U, V, A, B, T, Q, GX, GY, C = range(9)
MOVING = 5


def layout(count):
    deep = 2 * count
    widths = {U: deep, V: deep, A: deep - 1, T: deep - 1, Q: deep - 1, C: deep - 1}
    widths.update({B: deep - 2, GX: deep - 2, GY: deep - 2})
    for level in range(1, count):
        widths[C + level] = deep - 1 - 2 * level
    names = list(widths)

    def window(start, width):
        return {(start + i) % LANES for i in range(width)}

    def settle(index, to_west, to_east):
        if index == len(names):
            return {}
        width = widths[names[index]]
        for turn in range(LANES - width + 1):
            mine, other = window(turn, width), window(HALF + turn - width, width)
            if mine & to_west or other & to_east:
                continue
            rest = settle(index + 1, to_west | mine, to_east | other)
            if rest is not None:
                return {names[index]: (turn, (HALF + turn - width) % LANES), **rest}
            if index < len(names) - 3:
                return None
        free_west = [p for p in range(LANES - width + 1) if not window(p, width) & to_west]
        free_east = [p for p in range(LANES - width + 1) if not window(p, width) & to_east]
        if not free_west or not free_east:
            return None
        west, east = free_west[0], free_east[0]
        rest = settle(index + 1, to_west | window(west, width), to_east | window(east, width))
        return None if rest is None else {names[index]: (west, east), **rest}

    return widths, settle(0, set(), set())


def spin(cells, shift):
    shift = shift % LANES
    return cells if shift == 0 else pltpu.roll(cells, shift, 1)


def lay(lane, parts):
    parts = sorted(parts, key=lambda part: part[0])
    start, width, cells = parts[-1]
    total = cells if start + width > LANES else parts[0][2]
    for start, width, cells in parts:
        total = jnp.where(lane >= start, cells, total)
    return total


def stress(u_x, u_y, v_x, v_y, a, b, t, c, q):
    both = u_x + v_y
    next_a = KEEP * a + (c * (both + 2.0 * u_x) - q)
    next_b = KEEP * b + (c * (both + 2.0 * v_y) - q)
    return next_a, next_b, KEEP * t + c * (u_y + v_x)


def momentum(u, v, f_x, f_y, q, g_x, g_y):
    gain = jnp.where(q > 0.0, DAMP, 0.0)
    turn, push = STEP_WEIGHT * CORIOLIS, STEP_WEIGHT * 0.25
    next_u = gain * (u + (turn * v + push * f_x)) + g_x
    next_v = gain * (v + (push * f_y - turn * u)) + g_y
    return next_u, next_v


def finish(u, v, a, b, t):
    return u, v, 0.5 * (a + b), 0.5 * (a - b), 0.5 * t


def reaches(count, level, rows):
    reach = 2 * (count - 1 - level)

    def span(extra):
        low = (RIM - reach - extra) // SUBLANES
        high = -(-(RIM + rows + reach + extra) // SUBLANES)
        return range(low, high)

    return span(1), span(0)


def kernel(
    count,
    lats,
    lons,
    route_in,
    state,
    forcing,
    strength,
    mask,
    regime,
    flux,
    blocks,
    raw_state,
    raw_force,
    raw_strength,
    raw_mask,
    raw_regime,
    ext,
    pack_west,
    pack_east,
    rim_east,
    rim_west,
    work_u,
    work_v,
    work_a,
    work_b,
    work_t,
    side_u,
    side_v,
    side_a,
    side_b,
    side_t,
    side_fixed,
    sides,
    outbox,
    side_out,
    side_in,
    route,
    order,
    load_sem,
    rim_send,
    rim_recv,
    route_send,
    route_recv,
    side_send,
    side_recv,
    own_sem,
    ready,
):
    fields = C + count
    widths, places = layout(count)
    groups = state.shape[1]
    rows = groups * SUBLANES
    block_rows = rows // lats
    block_groups = block_rows // SUBLANES
    deep = 2 * count
    me = lax.axis_index("lat")
    here = lax.axis_index("lon")
    west = lax.rem(here + lons - 1, lons)
    east = lax.rem(here + 1, lons)
    north = lax.rem(me + lats - 1, lats)
    south = lax.rem(me + 1, lats)
    odd = lax.rem(here, 2)

    barrier = pltpu.get_barrier_semaphore()
    for step in range(1, lats):
        pl.semaphore_signal(
            barrier, inc=1, device_id=(lax.rem(me + step, lats), here), device_id_type=MESH
        )
    around = [(lat, lon) for lon in (west, east) for lat in (north, me, south)]

    loads = []

    def load(src, dst):
        copy = pltpu.make_async_copy(src, dst, load_sem.at[len(loads)])
        copy.start()
        loads.append(copy)

    def load_groups(at):
        first = len(loads)
        load(state.at[:, at], raw_state.at[:, at])
        load(forcing.at[:, at], raw_force.at[:, at])
        load(strength.at[at], raw_strength.at[at])
        load(mask.at[at], raw_mask.at[at])
        load(regime.at[:, at], raw_regime.at[:, at])
        return loads[first:]

    half = (groups - 2 * EDGE) // 2
    chunks = [
        load_groups(pl.ds(0, EDGE)),
        load_groups(pl.ds(groups - EDGE, EDGE)),
        load_groups(pl.ds(EDGE, half)),
        load_groups(pl.ds(EDGE + half, groups - 2 * EDGE - half)),
    ]
    load(route_in, route)

    lane = lax.broadcasted_iota(jnp.int32, (SUBLANES, LANES), 1)
    right_part = (lane >= HALF // 2) & (lane < HALF)

    def fold(left, right):
        return jnp.where(right_part, spin(right, HALF), left)

    side_moving = (side_u, side_v, side_a, side_b, side_t)

    def side_rows(group):
        row = (group + 1) * SUBLANES
        return pl.ds(row if isinstance(group, int) else pl.multiple_of(row, SUBLANES), SUBLANES)

    def put_side(field, group, cells):
        if field < MOVING:
            side_moving[field][side_rows(group), :] = cells
        else:
            side_fixed[field - MOVING, group] = cells

    def get_side(field, group):
        if field < MOVING:
            return side_moving[field][side_rows(group), :]
        return side_fixed[field - MOVING, group]

    def prepare(at, _):
        made = []
        for tile in range(2):
            lanes = pl.ds(tile * LANES, LANES)
            ice = raw_mask[at, :, lanes].astype(jnp.float32)
            firm = ice * raw_strength[at, :, lanes]
            s1 = ice * raw_state[2, at, :, lanes]
            s2 = ice * raw_state[3, at, :, lanes]
            push = (STEP_WEIGHT * DAMP) * ice
            low = firm * (KEEP * 0.125)
            cells = {
                U: raw_state[0, at, :, lanes],
                V: raw_state[1, at, :, lanes],
                A: s1 + s2,
                B: s1 - s2,
                T: (2.0 * ice) * raw_state[4, at, :, lanes],
                Q: firm * (KEEP * 0.5),
                GX: push * (raw_force[0, at, :, lanes] + DRAG_COEF * raw_force[2, at, :, lanes]),
                GY: push * (raw_force[1, at, :, lanes] + DRAG_COEF * raw_force[3, at, :, lanes]),
            }
            for level in range(count):
                stiff = 3.0 - 2.0 * raw_regime[level, at, :, lanes].astype(jnp.float32)
                cells[C + level] = low * stiff
            for field in range(fields):
                ext[field, tile, at + EDGE] = cells[field]
            made.append(cells)
        to_west, to_east = [], []
        for field, (start, other) in places.items():
            width = widths[field]
            both = fold(made[0][field], made[1][field])
            put_side(field, at + EDGE, both)
            moved = spin(both, start)
            to_west.append((start, width, moved))
            if other != (HALF + start - width) % LANES:
                moved = spin(both, other + width - HALF)
            to_east.append((other, width, moved))
        pack_west[at] = lay(lane, to_west)
        pack_east[at] = lay(lane, to_east)
        return 0

    def copies_done(chunk):
        for copy in chunk:
            copy.wait()

    copies_done(chunks[0] + chunks[1])
    for end in (0, groups - EDGE):
        for group in range(EDGE):
            prepare(end + group, 0)

    def rim_copy(index, src, dst, lat, lon):
        return pltpu.make_async_remote_copy(
            src_ref=src,
            dst_ref=dst,
            send_sem=rim_send.at[index],
            recv_sem=rim_recv.at[index],
            device_id=(lat, lon),
            device_id_type=MESH,
        )

    far = C + sum(1 for level in range(count) if deep - 1 - 2 * level > SUBLANES)
    near_count = fields - far
    top, bottom = pl.ds(0, EDGE), pl.ds(EDGE + groups, EDGE)
    first, last = pl.ds(0, EDGE), pl.ds(groups - EDGE, EDGE)
    wide_fields, late_fields = pl.ds(0, far), pl.ds(far, near_count)

    def lat_copy(index, part, src, dst, lat):
        return rim_copy(index, ext.at[part, :, src], ext.at[part, :, dst], lat, here)

    lat_ups = [
        lat_copy(0, wide_fields, pl.ds(EDGE, EDGE), bottom, north),
        lat_copy(1, late_fields, pl.ds(EDGE, 1), pl.ds(EDGE + groups, 1), north),
    ]
    lat_downs = [
        lat_copy(2, wide_fields, pl.ds(groups, EDGE), top, south),
        lat_copy(3, late_fields, pl.ds(groups + EDGE - 1, 1), pl.ds(EDGE - 1, 1), south),
    ]

    def lon_copies(index, start, size):
        src, dst = pl.ds(start, size), pl.ds(start + EDGE, size)
        return [
            rim_copy(index, pack_west.at[src], rim_east.at[dst], me, west),
            rim_copy(index + 1, pack_east.at[src], rim_west.at[dst], me, east),
        ]

    lon_early = lon_copies(4, 0, EDGE + half)
    lon_late = lon_copies(10, EDGE + half, groups - EDGE - half)
    lon_both = lon_early + lon_late
    lon_ups = [
        rim_copy(6, pack_west.at[first], rim_east.at[bottom], north, west),
        rim_copy(7, pack_east.at[first], rim_west.at[bottom], north, east),
    ]
    lon_downs = [
        rim_copy(8, pack_west.at[last], rim_east.at[top], south, west),
        rim_copy(9, pack_east.at[last], rim_west.at[top], south, east),
    ]
    has_north, has_south = me > 0, me < lats - 1

    @pl.when(odd == 0)
    def _():
        pl.semaphore_wait(barrier, lats - 1)

    @pl.when(odd == 1)
    def _():
        pl.semaphore_wait(barrier, lats - 1 + len(around))

    @pl.when(has_north)
    def _():
        for copy in lat_ups:
            copy.start()

    @pl.when(has_south)
    def _():
        for copy in lat_downs:
            copy.start()

    @pl.when(odd == 0)
    def _():
        for target in around:
            pl.semaphore_signal(barrier, inc=1, device_id=target, device_id_type=MESH)

    @pl.when(odd == 1)
    def _():
        for target in around:
            pl.semaphore_signal(ready, inc=1, device_id=target, device_id_type=MESH)

    def send_lon(part):
        for copy in part:
            copy.start()

    copies_done(chunks[2])
    lax.fori_loop(EDGE, EDGE + half, prepare, 0, unroll=7)

    @pl.when(odd == 1)
    def _():
        send_lon(lon_early)

    copies_done(chunks[3])
    lax.fori_loop(EDGE + half, groups - EDGE, prepare, 0, unroll=7)

    def send_corners():
        @pl.when(has_north)
        def _():
            for copy in lon_ups:
                copy.start()

        @pl.when(has_south)
        def _():
            for copy in lon_downs:
                copy.start()

    @pl.when(odd == 1)
    def _():
        send_lon(lon_late)
        send_corners()

    loads[-1].wait()
    for lat in range(lats):
        block = jnp.int32(0)
        for j in range(1, lats):
            apart = route[me, j] - lat
            block = block + j * (1 - lax.div(apart * apart + 63, 64))
        order[lat] = lax.rem(block, lats)

    def blank(at):
        nothing = jnp.zeros((EDGE, SUBLANES, LANES), jnp.float32)
        rim_east[at] = nothing
        rim_west[at] = nothing
        for field in range(fields):
            for tile in range(2):
                ext[field, tile, at] = nothing

    @pl.when(me == 0)
    def _():
        blank(top)

    @pl.when(me == lats - 1)
    def _():
        blank(bottom)

    line = jnp.zeros((SUBLANES, LANES), jnp.float32)
    for work in (work_u, work_v, work_a, work_b, work_t):
        for tile in range(2):
            work[tile, pl.ds(0, SUBLANES), :] = line
            work[tile, pl.ds(block_rows + 2 * RIM + SUBLANES, SUBLANES), :] = line
    for side in (side_u, side_v, side_a, side_b, side_t):
        side[pl.ds(0, SUBLANES), :] = line
        side[pl.ds(rows + 2 * RIM + SUBLANES, SUBLANES), :] = line

    @pl.when(has_south)
    def _():
        for copy in lat_ups:
            copy.wait_recv()

    @pl.when(has_north)
    def _():
        for copy in lat_downs:
            copy.wait_recv()

    core = lax.rem(me, 2)
    chip = me // 2
    chips = lats // 2

    def hop_of(step, core):
        sign = jnp.where(core == 0, 1, chips - 1)
        hop = jnp.where((step == 0) | (step == 4), sign, 0)
        hop = jnp.where((step == 1) | (step == 3), 2, hop)
        return jnp.where((step == 2) | (step == 5), chips - sign, hop)

    def swap_of(step):
        return jnp.where((step >= 3) & (step <= 6), 1, 0)

    def taker_of(step):
        lat_chip = lax.rem(chip + hop_of(step, core), chips)
        return lat_chip * 2 + lax.rem(core + swap_of(step), 2)

    def giver_of(step):
        other = lax.rem(core + swap_of(step), 2)
        return lax.rem(chip + chips - hop_of(step, other), chips) * 2 + other

    def route_copy(step, lat, slot):
        return pltpu.make_async_remote_copy(
            src_ref=outbox.at[lat],
            dst_ref=blocks.at[slot],
            send_sem=route_send.at[step],
            recv_sem=route_recv.at[step],
            device_id=(lat, here),
            device_id_type=MESH,
        )

    def side_copy(step, lat, slot):
        return pltpu.make_async_remote_copy(
            src_ref=side_out.at[lat],
            dst_ref=side_in.at[slot],
            send_sem=side_send.at[step],
            recv_sem=side_recv.at[step],
            device_id=(lat, here),
            device_id_type=MESH,
        )

    right_end = lane == LANES - 1
    left_end = lane == 0

    def across(tiles):
        ahead = [spin(cells, -1) for cells in tiles]
        behind = [spin(cells, 1) for cells in tiles]
        return [
            jnp.where(right_end, ahead[1 - t], ahead[t])
            - jnp.where(left_end, behind[1 - t], behind[t])
            for t in range(2)
        ]

    def around_row(group):
        row = (group + 1) * SUBLANES
        return [pl.ds(row + shift, SUBLANES) for shift in (0, 1, -1)]

    def subcycles(target):
        base = order[target] * block_groups

        def fixed(field, tile, group):
            return ext[field, tile, base + group]

        for group in range(block_groups + 2 * EDGE):
            at = around_row(group)[0]
            for tile in range(2):
                work_u[tile, at, :] = fixed(U, tile, group)
                work_v[tile, at, :] = fixed(V, tile, group)

        for level in range(count):
            stress_span, momentum_span = reaches(count, level, block_rows)
            for group in stress_span:
                at, over, under = around_row(group)
                u_x = across([work_u[t, at, :] for t in range(2)])
                v_x = across([work_v[t, at, :] for t in range(2)])
                for t in range(2):
                    u_y = work_u[t, over, :] - work_u[t, under, :]
                    v_y = work_v[t, over, :] - work_v[t, under, :]
                    if level == 0:
                        old = [fixed(field, t, group) for field in (A, B, T)]
                    else:
                        old = [work[t, at, :] for work in (work_a, work_b, work_t)]
                    c, q = fixed(C + level, t, group), fixed(Q, t, group)
                    new = stress(u_x[t], u_y, v_x[t], v_y, *old, c, q)
                    for work, cells in zip((work_a, work_b, work_t), new):
                        work[t, at, :] = cells
            final = level == count - 1
            for group in momentum_span:
                at, over, under = around_row(group)
                here_a = [work_a[t, at, :] for t in range(2)]
                here_t = [work_t[t, at, :] for t in range(2)]
                a_x, t_x = across(here_a), across(here_t)
                for t in range(2):
                    f_x = a_x[t] + (work_t[t, over, :] - work_t[t, under, :])
                    f_y = t_x[t] + (work_b[t, over, :] - work_b[t, under, :])
                    new = momentum(
                        work_u[t, at, :],
                        work_v[t, at, :],
                        f_x,
                        f_y,
                        fixed(Q, t, group),
                        fixed(GX, t, group),
                        fixed(GY, t, group),
                    )
                    if final:
                        done = finish(*new, here_a[t], work_b[t, at, :], here_t[t])
                        inside = pl.ds((group - EDGE) * SUBLANES, SUBLANES)
                        for part, cells in enumerate(done):
                            outbox[target, part, inside, pl.ds(t * LANES, LANES)] = cells
                    else:
                        work_u[t, at, :], work_v[t, at, :] = new

    partner_step = lats - 2
    held = range(partner_step - HELD, partner_step)

    answered = 2

    def deliver(step, _):
        lat = taker_of(step)

        @pl.when((odd == 0) & (step == answered))
        def _():
            pl.semaphore_wait(ready, len(around))
            send_lon(lon_both)
            send_corners()

        subcycles(lat)

        @pl.when((step < held[0]) | (step == partner_step))
        def _():
            route_copy(step, lat, me).start()

        return 0

    lax.fori_loop(0, lats - 2, deliver, 0)

    for copy in lon_both:
        copy.wait_recv()

    @pl.when(has_south)
    def _():
        for copy in lon_ups:
            copy.wait_recv()

    @pl.when(has_north)
    def _():
        for copy in lon_downs:
            copy.wait_recv()

    def unpack(group, names, beyond):
        from_east, from_west = rim_east[group], rim_west[group]
        for field in names:
            start, other = places[field]
            width = widths[field]
            if other == (HALF + start - width) % LANES:
                end = (start + HALF // 2) % LANES
                if start < end:
                    mine = (lane >= start) & (lane < end)
                else:
                    mine = (lane >= start) | (lane < end)
                rim = spin(jnp.where(mine, from_east, from_west), HALF - start)
            else:
                rim = jnp.where(
                    lane < LANES - HALF // 2,
                    spin(from_east, HALF - start),
                    spin(from_west, -other - width),
                )
            if beyond:
                base = fold(ext[field, 0, group], ext[field, 1, group])
            else:
                base = get_side(field, group)
            put_side(field, group, jnp.where(lane < HALF, base, rim))

    for group in (0, groups + 2 * EDGE - 1):
        unpack(group, range(far), True)
    for group in (1, groups + 2 * EDGE - 2):
        unpack(group, range(fields), True)

    def unpack_inside(group, _):
        unpack(group, range(fields), False)
        return 0

    lax.fori_loop(EDGE, groups + EDGE, unpack_inside, 0, unroll=8)

    def beside(cells):
        return spin(cells, -1) - spin(cells, 1)

    def middle_of(part):
        return 2 * deep * part + deep

    for level in range(count):
        stress_span, momentum_span = reaches(count, level, rows)
        for group in stress_span:
            at, over, under = around_row(group)
            new = stress(
                beside(side_u[at, :]),
                side_u[over, :] - side_u[under, :],
                beside(side_v[at, :]),
                side_v[over, :] - side_v[under, :],
                side_a[at, :],
                side_b[at, :],
                side_t[at, :],
                side_fixed[C + level - MOVING, group],
                side_fixed[Q - MOVING, group],
            )
            side_a[at, :], side_b[at, :], side_t[at, :] = new
        for group in momentum_span:
            at, over, under = around_row(group)
            a, b, t = side_a[at, :], side_b[at, :], side_t[at, :]
            new = momentum(
                side_u[at, :],
                side_v[at, :],
                beside(a) + (side_t[over, :] - side_t[under, :]),
                beside(t) + (side_b[over, :] - side_b[under, :]),
                side_fixed[Q - MOVING, group],
                side_fixed[GX - MOVING, group],
                side_fixed[GY - MOVING, group],
            )
            if level < count - 1:
                side_u[at, :], side_v[at, :] = new
            else:
                parts = []
                for part, cells in enumerate(finish(*new, a, b, t)):
                    cells = jnp.where(lane < HALF // 2, cells, spin(cells, HALF))
                    start = middle_of(part) - deep
                    parts.append((start, 2 * deep, spin(cells, middle_of(part))))
                sides[group - EDGE] = lay(lane, parts)

    def deliver_sides(step, _):
        lat = taker_of(step)
        base = order[lat] * block_groups
        for group in range(block_groups):
            side_out[lat, group] = sides[base + group]

        @pl.when((step < held[0]) | (step == partner_step))
        def _():
            side_copy(step, lat, me).start()

        return 0

    lax.fori_loop(0, lats, deliver_sides, 0)

    def place(packed, part, tiles):
        moved = spin(packed, -middle_of(part))
        return (
            jnp.where(lane < deep, moved, tiles[0]),
            jnp.where(lane >= LANES - deep, moved, tiles[1]),
        )

    both_lanes = [pl.ds(tile * LANES, LANES) for tile in range(2)]

    def mend(whole, slot, source):
        for group in range(block_groups):
            packed = source[slot, group]
            at = pl.ds(group * SUBLANES, SUBLANES)
            for part in range(MOVING):
                tiles = place(packed, part, [whole[slot, part, at, lanes] for lanes in both_lanes])
                for lanes, cells in zip(both_lanes, tiles):
                    whole[slot, part, at, lanes] = cells

    for step in held:
        mend(outbox, taker_of(step), side_out)
        route_copy(step, taker_of(step), me).start()
    lax.fori_loop(lats - 2, lats, deliver, 0)

    own = pltpu.make_async_copy(outbox.at[me], blocks.at[me], own_sem)
    own.start()

    def exchange(j, _):
        taker = route[me, j]
        for part in range(block_groups):
            at = pl.ds(part * SUBLANES, SUBLANES)
            group = j * block_groups + part
            row = pl.multiple_of(group * SUBLANES, SUBLANES)
            for axis in range(2):
                drift = [outbox[taker, axis, at, lanes] for lanes in both_lanes]
                drift = place(sides[group], axis, drift)
                for tile, lanes in enumerate(both_lanes):
                    icy = ext[Q, tile, group + EDGE] > 0.0
                    moved = drift[tile] - raw_force[2 + axis, group, :, lanes]
                    flux[axis, pl.ds(row, SUBLANES), lanes] = jnp.where(icy, DRAG_COEF * moved, 0.0)
        return 0

    lax.fori_loop(0, lats, exchange, 0)

    own.wait()
    mend(blocks, me, side_out)

    def receive(turn, _):
        step = jnp.where(turn < held[0], turn, partner_step)
        lat = giver_of(step)
        route_copy(step, lat, lat).wait_recv()
        side_copy(step, lat, lat).wait_recv()
        mend(blocks, lat, side_in)
        return 0

    lax.fori_loop(0, held[0] + 1, receive, 0)
    for step in held:
        route_copy(step, giver_of(step), giver_of(step)).wait_recv()

    def settle(turn, _):
        step = jnp.where(turn < held[0], turn, partner_step)
        route_copy(step, taker_of(step), me).wait_send()
        side_copy(step, taker_of(step), me).wait_send()
        return 0

    lax.fori_loop(0, held[0] + 1, settle, 0)
    for step in held:
        route_copy(step, taker_of(step), me).wait_send()

    for copy in lon_both:
        copy.wait_send()

    @pl.when(has_north)
    def _():
        for copy in lat_ups + lon_ups:
            copy.wait_send()

    @pl.when(has_south)
    def _():
        for copy in lat_downs + lon_downs:
            copy.wait_send()


def hand_out(flux, blocks, flux_out, blocks_out, sems):
    copies = [
        pltpu.make_async_copy(flux, flux_out, sems.at[0]),
        pltpu.make_async_copy(blocks, blocks_out, sems.at[1]),
    ]
    for copy in copies:
        copy.start()
    for copy in copies:
        copy.wait()


def per_device(lats, lons, ice_state, ocean_forcing, ice_strength, ice_mask, yield_mask, ice_route):
    count, rows, columns = yield_mask.shape
    block_rows = rows // lats
    fields = C + count
    groups = rows // SUBLANES
    f32, i32 = jnp.float32, jnp.int32
    as_is = pl.BlockSpec(memory_space=pl.ANY)
    vmem = pl.BlockSpec(memory_space=pltpu.VMEM)
    dma = pltpu.SemaphoreType.DMA

    def tiles(*lead, kind=f32, wide=LANES):
        return pltpu.VMEM(lead + (SUBLANES, wide), kind)

    def split(cells):
        return cells.reshape(cells.shape[:-2] + (groups, SUBLANES, columns))

    work = pltpu.VMEM((2, block_rows + 2 * RIM + 2 * SUBLANES, LANES), f32)
    side = pltpu.VMEM((rows + 2 * RIM + 2 * SUBLANES, LANES), f32)
    shapes = ((2, rows, columns), (lats, 5, block_rows, columns))
    results = pl.pallas_call(
        functools.partial(kernel, count, lats, lons),
        out_shape=tuple(pltpu.VMEM(shape, f32) for shape in shapes),
        in_specs=[as_is] * 6,
        out_specs=(vmem, vmem),
        scratch_shapes=[
            tiles(5, groups, wide=columns),
            tiles(4, groups, wide=columns),
            tiles(groups, wide=columns),
            tiles(groups, kind=i32, wide=columns),
            tiles(count, groups, kind=i32, wide=columns),
            tiles(fields, 2, groups + 2 * EDGE),
            tiles(groups),
            tiles(groups),
            tiles(groups + 2 * EDGE),
            tiles(groups + 2 * EDGE),
            work,
            work,
            work,
            work,
            work,
            side,
            side,
            side,
            side,
            side,
            tiles(fields - MOVING, groups + 2 * EDGE),
            tiles(groups),
            pltpu.VMEM((lats, 5, block_rows, columns), f32),
            tiles(lats, block_rows // SUBLANES),
            tiles(lats, block_rows // SUBLANES),
            pltpu.SMEM((lats, lats), i32),
            pltpu.SMEM((lats,), i32),
            dma((21,)),
            dma((12,)),
            dma((12,)),
            dma((lats - 1,)),
            dma((lats - 1,)),
            dma((lats - 1,)),
            dma((lats - 1,)),
            dma,
            pltpu.SemaphoreType.REGULAR,
        ],
        compiler_params=pltpu.CompilerParams(collective_id=0, has_side_effects=True),
        name="ice_step",
    )(
        ice_route,
        split(ice_state),
        split(ocean_forcing),
        split(ice_strength),
        split(ice_mask),
        split(yield_mask),
    )
    return pl.pallas_call(
        hand_out,
        out_shape=tuple(jax.ShapeDtypeStruct(shape, f32) for shape in shapes),
        in_specs=[as_is] * 2,
        out_specs=(as_is, as_is),
        scratch_shapes=[dma((2,))],
        compiler_params=pltpu.CompilerParams(vmem_limit_bytes=1 << 20),
        name="hand_out",
    )(*results)


def solution(mesh):
    return jax.shard_map(
        functools.partial(per_device, mesh.shape["lat"], mesh.shape["lon"]),
        mesh=mesh,
        in_specs=(
            P(None, "lat", "lon"),
            P(None, "lat", "lon"),
            P("lat", "lon"),
            P("lat", "lon"),
            P(None, "lat", "lon"),
            P(),
        ),
        out_specs=(P(None, "lat", "lon"), P("lat", None, None, "lon")),
        check_vma=False,
    )
```
